512 devices in a mesh: dp: 32 (over z, core), seq: 16 (over y, x).
Axes of the slice: x: 4, y: 4, z: 16, core: 2. Of those that a mesh axis runs over, the one named last changes fastest.
Arguments:
- q_pre: bfloat16 [32, 2048, 16, 128], P('dp', 'seq'), may hold values from -6 to 6
- k_pre: bfloat16 [32, 2048, 8, 128], P('dp', 'seq'), may hold values from -6 to 6
- values: bfloat16 [32, 2048, 8, 128], P('dp', 'seq'), may hold values from -6 to 6
- grad_out: bfloat16 [32, 2048, 16, 128], P('dp', 'seq'), may hold values from -6 to 6
- segment_ids: int32 [32, 2048], P('dp', 'seq'), may hold values from 0 to 7, never falling along the last dimension, each value on 1 to 1024 neighbouring positions
- q_gain: float32 [128], replicated, may hold values from 0.1 to 1.9
- k_gain: float32 [128], replicated, may hold values from 0.1 to 1.9
Outputs:
- grad_q: bfloat16 [32, 2048, 16, 128], P('dp', 'seq')
- grad_k: bfloat16 [32, 2048, 8, 128], P('dp', 'seq')
- grad_v: bfloat16 [32, 2048, 8, 128], P('dp', 'seq')
- grad_q_gain: float32 [128], replicated
- grad_k_gain: float32 [128], replicated
The draws below stay inside these ranges and needn't reach their ends.
Inputs may be any that keep to these rules, and one draw needn't show every extreme that they name: `segment_ids`: along a span the ids never fall, and each id from 0 to 7 names one run of consecutive tokens.
All inputs are finite; a program needn't handle non-finite values.
Results may differ from the reference program's by a relative error of at most 0.017.
Values may be sent and summed in bfloat16 or wider, within the bound.
A program may use at most 64 MiB of HBM per device.

```python
import math
import jax
import jax.numpy as jnp
import numpy as np
from jax import lax

QH = 16
KVH = 8
HD = 128
PRESCALE = 168
DOCS = 8
SPANS = 32
SEQLEN = 2048


def shard_levels(key, extent, shards, smallest, high):
    def one(axis_at, blocks):
        steps = jax.random.uniform(jax.random.fold_in(jax.random.fold_in(key, 6), axis_at), (blocks,), jnp.float32, smallest / len(shards), high / len(shards))
        return jnp.repeat(jnp.exp(steps), extent[axis_at] // blocks).reshape((-1,) + (1,) * (len(extent) - axis_at - 1))

    loudness = one(*shards[0])
    for cut in shards[1:]:
        loudness = loudness * one(*cut)
    return loudness


def split_up(count, total, limit, slope):
    portions = [(1 << 20) // math.isqrt(grade ** slope) + 1 for grade in range(2, count + 1)]
    spare, holding = total - limit - (count - 1), [1] * (count - 1)
    while spare > 0:
        candidates = [i for i in range(count - 1) if holding[i] < limit]
        pool, left = sum([portions[i] for i in candidates]), spare
        for i in candidates:
            addition = min(limit - holding[i], max(1, left * portions[i] // pool), spare)
            holding[i] = holding[i] + addition
            spare = spare - addition
    return np.array([limit] + holding)


def ragged(own_key, number_of, total, reach, skew):
    if number_of == 2:
        one = jax.random.randint(own_key, (), max(1, total - reach), min(reach, total - 1) + 1)
        return jnp.stack([one, total - one])
    lengths = jnp.asarray(split_up(number_of, total, reach, skew), jnp.int32)
    couples = (number_of - 1) // 2
    source_of, sink = lengths[1:1 + 2 * couples:2], lengths[2:2 + 2 * couples:2]
    room = jnp.minimum(source_of - 1, reach - sink)
    shifted = jax.random.randint(jax.random.fold_in(own_key, 1), (couples,), 0, 1 << 20) % (room + 1)
    lengths = lengths.at[1:1 + 2 * couples:2].set(source_of - shifted).at[2:2 + 2 * couples:2].set(sink + shifted)
    return lengths[jax.random.permutation(jax.random.fold_in(own_key, 2), number_of)]


def gaussian(key, shape, scale, bound, cuts=(), kind=jnp.bfloat16):
    array = scale * jax.random.normal(key, shape, jnp.float32)
    if cuts:
        array = array * shard_levels(key, shape, cuts, -0.22, 0.18)
    return jnp.clip(array, -bound, bound).astype(kind)


def setup_inputs(seed: int = 0) -> dict:
    key_list = jax.random.split(jax.random.key(seed), 8)
    return {
        "q_pre": gaussian(key_list[0], (SPANS, SEQLEN, QH, HD), 1.0, 6.0, ((0, 32), (1, 16))),
        "k_pre": gaussian(key_list[1], (SPANS, SEQLEN, KVH, HD), 1.0, 6.0, ((0, 32), (1, 16))),
        "values": gaussian(key_list[2], (SPANS, SEQLEN, KVH, HD), 1.0, 6.0, ((0, 32), (1, 16))),
        "grad_out": gaussian(key_list[3], (SPANS, SEQLEN, QH, HD), 1.0, 6.0, ((0, 32), (1, 16))),
        "segment_ids": jax.vmap(lambda own: jnp.searchsorted(jnp.cumsum(ragged(own, DOCS, SEQLEN, SEQLEN // 2, 2)), jnp.arange(SEQLEN), side="right"))(jax.random.split(key_list[4], SPANS)).reshape((SPANS, SEQLEN)).astype(jnp.int32),
        "q_gain": jnp.clip(1.0 + 0.18 * jax.random.normal(key_list[5], (HD,), jnp.float32), 0.1, 1.9),
        "k_gain": jnp.clip(1.0 + 0.18 * jax.random.normal(key_list[6], (HD,), jnp.float32), 0.1, 1.9),
    }


norm_epsilon = 1e-06
rope_base = 1000000.0
rope_factor = 8.0

def document_positions(segments, docs):
    labels = jnp.arange(docs, dtype=jnp.int32)
    member = (segments[:, None] == labels[None, :]).astype(jnp.int32)
    counts = lax.optimization_barrier(jnp.sum(member, axis=0)).astype(jnp.int32)
    starts = (jnp.cumsum(counts) - counts).astype(jnp.int32)
    first = lax.optimization_barrier(jnp.sum(member * starts[None, :], axis=1)).astype(jnp.int32)
    return (jnp.arange(segments.shape[0], dtype=jnp.int32) - first, first)

def embed(rows, gain, positions):
    width = rows.shape[-1]
    half = width // 2
    scale = lax.rsqrt(lax.optimization_barrier(jnp.mean(rows * rows, axis=-1, keepdims=True)) + norm_epsilon)
    normed = rows * scale * gain
    freqs = rope_base ** (-(jnp.arange(half, dtype=jnp.float32) * 2.0 / width))
    angles = (positions.astype(jnp.float32) / rope_factor)[:, None] * freqs[None, :]
    cosine = jnp.cos(angles)[:, None, :]
    sine = jnp.sin(angles)[:, None, :]
    first_half = normed[..., :half]
    second_half = normed[..., half:]
    return jnp.concatenate([first_half * cosine - second_half * sine, second_half * cosine + first_half * sine], axis=-1)

def attend(queries, keys, vals, upstream, visible, score_scale):
    group_queries = jnp.transpose(queries, (1, 0, 2)).astype(jnp.float32)
    key_rows = keys.astype(jnp.float32)
    value_rows = vals.astype(jnp.float32)
    scores = score_scale * jnp.einsum('gid,jd->gij', group_queries, key_rows)
    raw = jnp.where(visible[None], jnp.exp(scores), 0.0)
    totals = lax.optimization_barrier(jnp.sum(raw, axis=-1))
    expo = lax.optimization_barrier(raw.astype(jnp.bfloat16)).astype(jnp.float32)
    outputs = jnp.einsum('gij,jd->gid', expo, value_rows) / totals[..., None]
    grads = jnp.transpose(upstream, (1, 0, 2)).astype(jnp.float32)
    delta = lax.optimization_barrier(jnp.sum(grads * outputs, axis=-1))
    logsum = jnp.log(totals)
    probs = jnp.where(visible[None], jnp.exp(scores - logsum[..., None]), 0.0)
    probs = lax.optimization_barrier(probs.astype(jnp.bfloat16)).astype(jnp.float32)
    value_grad = jnp.einsum('gij,gid->jd', probs, grads)
    prob_grads = jnp.einsum('gid,jd->gij', grads, value_rows)
    score_grads = (probs * (prob_grads - delta[..., None]) * score_scale).astype(jnp.bfloat16)
    score_grads = lax.optimization_barrier(score_grads).astype(jnp.float32)
    query_grad = jnp.einsum('gij,jd->gid', score_grads, key_rows)
    key_grad = jnp.einsum('gij,gid->jd', score_grads, group_queries)
    return (jnp.transpose(query_grad, (1, 0, 2)), key_grad, value_grad)

def reference(q_pre, k_pre, values, grad_out, segment_ids, q_gain, k_gain):
    total = q_pre.shape[1]
    heads = q_pre.shape[2]
    kv_heads = k_pre.shape[2]
    width = q_pre.shape[3]
    group = heads // kv_heads
    score_scale = float(PRESCALE) ** (-0.5)

    def one_span(inputs):
        queries, keys, vals, upstream, segments = inputs
        positions, first = document_positions(segments, DOCS)
        index = jnp.arange(total, dtype=jnp.int32)
        visible = (segments[:, None] == segments[None, :]) & (index[:, None] >= index[None, :])

        def embed_rows(rows, gain):
            return embed(rows, gain, positions)
        query_rot, query_back = jax.vjp(embed_rows, queries.astype(jnp.float32), q_gain)
        key_rot, key_back = jax.vjp(embed_rows, keys.astype(jnp.float32), k_gain)
        query_heads = query_rot.astype(jnp.bfloat16).reshape(total, kv_heads, group, width).transpose(1, 0, 2, 3)
        key_heads = key_rot.astype(jnp.bfloat16).transpose(1, 0, 2)
        value_heads = vals.transpose(1, 0, 2)
        upstream_heads = upstream.reshape(total, kv_heads, group, width).transpose(1, 0, 2, 3)

        def one_head(items):
            return attend(items[0], items[1], items[2], items[3], visible, score_scale)
        query_grad, key_grad, value_grad = lax.map(one_head, (query_heads, key_heads, value_heads, upstream_heads))
        query_grad = query_grad.transpose(1, 0, 2, 3).reshape(total, heads, width)
        key_grad = key_grad.transpose(1, 0, 2)
        query_input, query_gain_grad = query_back(query_grad)
        key_input, key_gain_grad = key_back(key_grad)
        return (query_input.astype(jnp.bfloat16), key_input.astype(jnp.bfloat16), value_grad.transpose(1, 0, 2).astype(jnp.bfloat16), query_gain_grad, key_gain_grad)
    grad_q, grad_k, grad_v, query_gains, key_gains = lax.map(one_span, (q_pre, k_pre, values, grad_out, segment_ids))
    return (grad_q, grad_k, grad_v, lax.optimization_barrier(jnp.sum(query_gains, axis=0)), lax.optimization_barrier(jnp.sum(key_gains, axis=0)))
```

```python
import functools

import jax
import jax.numpy as jnp
import numpy as np
from jax import lax
from jax.experimental import pallas as pl
from jax.experimental.pallas import tpu as pltpu
from jax.sharding import PartitionSpec as P

PRESCALE = 168
HD = 128
SEQ = 16
TOK = 128
TOTAL = SEQ * TOK
BLK = 256
NBLK = TOTAL // BLK
BAND = 5
EPS = 1e-6
ROPE_BASE = 1000000.0
ROPE_FACTOR = 8.0
SCALE = float(PRESCALE) ** (-0.5)
QMUL = SCALE * float(np.log2(np.e))
LN2 = float(np.log(2.0))
MESH = pl.DeviceIdType.MESH
F32 = jnp.float32
BF16 = jnp.bfloat16
ANY = pl.BlockSpec(memory_space=pl.ANY)
VM = pl.BlockSpec(memory_space=pltpu.VMEM)


def rope_tables():
    half = HD // 2
    freqs = ROPE_BASE ** (-(np.arange(half, dtype=np.float64) * 2.0 / HD))
    freqs = np.concatenate([freqs, freqs])
    near = np.arange(TOK, dtype=np.float64)[:, None] / ROPE_FACTOR * freqs[None, :]
    far = np.arange(SEQ, dtype=np.float64)[:, None] * TOK / ROPE_FACTOR * freqs[None, :]
    return (
        np.stack([np.cos(near), np.sin(near)]).astype(np.float32),
        np.stack([np.cos(far), np.sin(far)], axis=1).astype(np.float32),
    )


def block_rope(near_ref, far_ref, block):
    far = far_ref[block]
    cb, sb = far[0:1, :], far[1:2, :]
    cosine = near_ref[0] * cb - near_ref[1] * sb
    sine = near_ref[1] * cb + near_ref[0] * sb
    lane = lax.broadcasted_iota(jnp.int32, (TOK, HD), 1)
    return cosine, jnp.where(lane < HD // 2, -sine, sine)


def turn(rows, cosine, sine):
    return rows * cosine + pltpu.roll(rows, HD // 2, 1) * sine


def turn_back(rows, cosine, sine):
    return rows * cosine - pltpu.roll(rows, HD // 2, 1) * sine


def place():
    dp = lax.axis_index("dp")
    s = lax.axis_index("seq")
    z = lax.div(dp, 2)
    return dp, s, z, lax.rem(dp, 2)


def greet(z, dp, s, core):
    barrier = pltpu.get_barrier_semaphore()

    def one(i, carry):
        peer_core, peer_seq = lax.div(i, SEQ), lax.rem(i, SEQ)

        @pl.when((peer_core != core) | (peer_seq != s))
        def _():
            pl.semaphore_signal(
                barrier, inc=1, device_id=(2 * z + peer_core, peer_seq), device_id_type=MESH
            )

        return carry

    lax.fori_loop(0, 2 * SEQ, one, 0)
    return barrier


def gather_kernel(
    q_hbm, k_hbm, v_hbm, g_hbm, seg_ref, qg_ref, kg_ref, near_ref, far_ref,
    q_out, g_out, kv_out, seg_out,
    q_raw, k_raw, v_raw, g_raw, q_wide, k_wide, v_wide, g_wide, q_buf, g_buf, kv_buf,
    load_sem, send_sem, recv_sem, pass_send, pass_recv,
):
    dp, s, z, core = place()
    loads = [
        pltpu.make_async_copy(src, dst, load_sem.at[i])
        for i, (src, dst) in enumerate(
            ((g_hbm, g_raw), (v_hbm, v_raw), (k_hbm, k_raw), (q_hbm, q_raw))
        )
    ]
    for copy in loads:
        copy.start()
    barrier = greet(z, dp, s, core)
    pl.semaphore_wait(barrier, 2 * SEQ - 1)

    def copies(kind, src, dst, j, r):
        peer_dp, peer_seq = 2 * z + r, 2 * j + core
        me = (peer_dp == dp) & (peer_seq == s)
        remote = pltpu.make_async_remote_copy(
            src_ref=src, dst_ref=dst, send_sem=send_sem.at[kind, 2 * j + r],
            recv_sem=recv_sem.at[kind, s], device_id=(peer_dp, peer_seq), device_id_type=MESH,
        )
        local = pltpu.make_async_copy(src, dst, recv_sem.at[kind, s])
        return me, remote, local

    def send(kind, src, dst, j, r):
        me, remote, local = copies(kind, src, dst, j, r)

        @pl.when(me)
        def _():
            local.start()

        @pl.when(jnp.logical_not(me))
        def _():
            remote.start()

    def sent(kind, src, dst, j, r):
        me, remote, local = copies(kind, src, dst, j, r)

        @pl.when(jnp.logical_not(me))
        def _():
            remote.wait_send()

    def turns(t):
        return lax.rem(lax.div(s, 2) + t, SEQ // 2)

    def parts(j, r):
        h = 2 * j + r
        return (
            (0, g_buf.at[h], g_out.at[s]),
            (1, kv_buf.at[r, j], kv_out.at[r, s]),
            (2, q_buf.at[h], q_out.at[s]),
            (3, seg_ref, seg_out.at[s]),
        )

    loads[0].wait()
    g_wide[...] = g_raw[...].astype(F32).reshape(TOK * 16, HD)

    def send_g(t, carry):
        j = turns(t)
        for r in range(2):
            h = 2 * j + r
            g_buf[h] = g_wide[pl.ds(h, TOK, stride=16), :].astype(BF16)
            send(*parts(j, r)[3], j, r)
            send(*parts(j, r)[0], j, r)
        return carry

    lax.fori_loop(0, 8, send_g, 0)
    cosine, sine = block_rope(near_ref, far_ref, s)
    loads[1].wait()
    v_wide[...] = v_raw[...].astype(F32).reshape(TOK * 8, HD)
    loads[2].wait()
    k_wide[...] = k_raw[...].astype(F32).reshape(TOK * 8, HD)

    def send_kv(t, carry):
        j = turns(t)
        rows = k_wide[pl.ds(j, TOK, stride=8), :]
        size = lax.rsqrt(jnp.mean(rows * rows, axis=1, keepdims=True) + EPS)
        kv_buf[0, j] = turn(rows * size * kg_ref[...], cosine, sine).astype(BF16)
        send(*parts(j, 0)[1], j, 0)
        kv_buf[1, j] = v_wide[pl.ds(j, TOK, stride=8), :].astype(BF16)
        send(*parts(j, 1)[1], j, 1)
        return carry

    lax.fori_loop(0, 8, send_kv, 0)
    loads[3].wait()
    q_wide[...] = q_raw[...].astype(F32).reshape(TOK * 16, HD)

    def send_q(t, carry):
        j = turns(t)
        for r in range(2):
            h = 2 * j + r
            rows = q_wide[pl.ds(h, TOK, stride=16), :]
            size = lax.rsqrt(jnp.mean(rows * rows, axis=1, keepdims=True) + EPS)
            q_buf[h] = (turn(rows * size * qg_ref[...], cosine, sine) * QMUL).astype(BF16)
            send(*parts(j, r)[2], j, r)
        return carry

    lax.fori_loop(0, 8, send_q, 0)

    def passing(kind, t):
        return pltpu.make_async_remote_copy(
            src_ref=kv_out.at[kind, t], dst_ref=kv_out.at[kind, t],
            send_sem=pass_send.at[t], recv_sem=pass_recv.at[t],
            device_id=(2 * z + 1 - core, s), device_id_type=MESH,
        )

    def arrival(kind, ref):
        return pltpu.make_async_copy(ref, ref, recv_sem.at[kind[0], kind[1]])

    def forward(i, carry):
        t = lax.rem(s + i, SEQ)
        arrival((1, t), kv_out.at[core, t]).wait()
        passing(core, t).start()
        return carry

    lax.fori_loop(0, SEQ, forward, 0)

    def finish(t, carry):
        arrival((0, t), g_out.at[t]).wait()
        arrival((2, t), q_out.at[t]).wait()
        arrival((3, t), seg_out.at[t]).wait()
        passing(core, t).wait_send()
        passing(1 - core, t).wait_recv()
        return carry

    lax.fori_loop(0, SEQ, finish, 0)

    def drain(j, carry):
        for r in range(2):
            for part in parts(j, r):
                sent(*part, j, r)
        return carry

    lax.fori_loop(0, 8, drain, 0)


def attend_kernel(
    q_ref, g_ref, kv_ref, seg_ref, near_ref, far_ref,
    dq_ref, dkv_ref, gain_ref,
    expo, pgrad, dk_acc, dv_acc, first_ref, dqt_acc,
):
    seg = seg_ref[...].reshape(SEQ, TOK)
    first = jnp.zeros((SEQ, TOK), F32)
    for d in range(1, 8):
        below = jnp.where(seg < d, 1.0, 0.0)
        count = jnp.sum(jnp.sum(below, axis=1, keepdims=True), axis=0, keepdims=True)
        first = jnp.where(seg == d, count, first)
    first_ref[...] = first.astype(jnp.int32)
    dk_acc[...] = jnp.zeros_like(dk_acc)
    dv_acc[...] = jnp.zeros_like(dv_acc)
    last = (((1,), (1,)), ((), ()))
    key_at = lax.broadcasted_iota(jnp.int32, (BLK, BLK), 0)
    query_at = lax.broadcasted_iota(jnp.int32, (BLK, BLK), 1)
    low_lane = lax.broadcasted_iota(jnp.int32, (1, TOK), 1)
    gain_q = jnp.zeros((8, HD), F32)

    for qi in range(NBLK):
        start = qi * BLK
        queries = q_ref[2 * qi:2 * qi + 2].reshape(BLK, HD)
        upstream = g_ref[2 * qi:2 * qi + 2].reshape(BLK, HD)
        firsts = jnp.concatenate(
            [first_ref[2 * qi:2 * qi + 1, :], first_ref[2 * qi + 1:2 * qi + 2, :]], axis=1
        )
        low = jnp.min(first[2 * qi:2 * qi + 1, :]).astype(jnp.int32)
        low = jnp.maximum(lax.div(low, BLK), max(0, qi - BAND + 1))

        def rows_of(kind, kb):
            return kv_ref[kind, pl.ds(2 * kb, 2)].reshape(BLK, HD)

        def scores(kb, diagonal, state):
            total, mixed = state
            slot = kb - max(0, qi - BAND + 1)
            st = lax.dot_general(rows_of(0, kb), queries, last, preferred_element_type=F32)
            dpt = lax.dot_general(rows_of(1, kb), upstream, last, preferred_element_type=F32)
            seen = key_at >= firsts - kb * BLK
            if diagonal:
                seen = seen & (key_at <= query_at)
            e = jnp.where(seen, jnp.exp2(st), 0.0)
            expo[slot] = e
            pgrad[slot] = dpt
            total = total + jnp.sum(e.reshape(BLK // 8, 8, BLK), axis=0)
            mixed = mixed + jnp.sum((e * dpt).reshape(BLK // 8, 8, BLK), axis=0)
            return total, mixed

        zero = jnp.zeros((8, BLK), F32)
        state = lax.fori_loop(
            low, qi, lambda kb, state: scores(kb, False, state), (zero, zero)
        )
        total, mixed = scores(qi, True, state)
        inv = 1.0 / jnp.sum(total, axis=0, keepdims=True)
        delta = jnp.sum(mixed, axis=0, keepdims=True) * inv
        dqt_acc[...] = jnp.zeros_like(dqt_acc)

        def grads(kb, carry):
            slot = kb - max(0, qi - BAND + 1)
            p = expo[slot] * inv
            ds = (p * (pgrad[slot] - delta)).astype(BF16)
            p = p.astype(BF16)
            rows = pl.ds(pl.multiple_of(kb * BLK, BLK), BLK)
            dv_acc[rows, :] += jnp.dot(p, upstream, preferred_element_type=F32)
            dk_acc[rows, :] += jnp.dot(ds, queries, preferred_element_type=F32)
            dqt_acc[...] += lax.dot_general(
                ds, rows_of(0, kb), (((0,), (0,)), ((), ())), preferred_element_type=F32
            )
            return carry

        lax.fori_loop(low, qi + 1, grads, 0)
        dq = dqt_acc[...] * SCALE
        for half in range(2):
            block = 2 * qi + half
            rows = dq[half * TOK:(half + 1) * TOK, :]
            dq_ref[block] = rows.astype(BF16)
            cosine, sine = block_rope(near_ref, far_ref, block)
            both = turn_back(rows, cosine, sine) * turn_back(
                q_ref[block].astype(F32), cosine, sine
            )
            gain_q = gain_q + jnp.sum(both.reshape(TOK // 8, 8, HD), axis=0)

    def keys_out(block, gain_k):
        rows = pl.ds(pl.multiple_of(block * TOK, TOK), TOK)
        dk = dk_acc[rows, :] * LN2
        dkv_ref[0, block] = dk.astype(BF16)
        dkv_ref[1, block] = dv_acc[rows, :].astype(BF16)
        cosine, sine = block_rope(near_ref, far_ref, block)
        both = turn_back(dk, cosine, sine) * turn_back(
            kv_ref[0, block].astype(F32), cosine, sine
        )
        return gain_k + jnp.sum(both.reshape(TOK // 8, 8, HD), axis=0)

    gain_k = lax.fori_loop(0, SEQ, keys_out, jnp.zeros((8, HD), F32))
    row = lax.broadcasted_iota(jnp.int32, (8, HD), 0)
    gain_ref[...] = jnp.where(
        row == 0,
        jnp.sum(gain_q, axis=0, keepdims=True),
        jnp.where(row == 1, jnp.sum(gain_k, axis=0, keepdims=True), 0.0),
    )


def scatter_kernel(
    dq_hbm, dkv_hbm, gain_ref,
    dq_out, dkv_out, gain_out,
    mate, own, mine, along_z, plane, z_sum,
    load_sem, send_sem, recv_sem, pass_send, pass_recv, zs, zr, ps, pr,
):
    dp, s, z, core = place()
    span = lax.rem(s, 2)
    j = lax.div(s, 2)
    slot_q = 2 * j + core
    slot_kv = core * 8 + j
    other = (2 * z + 1 - core, s)
    load = pltpu.make_async_copy(dkv_hbm.at[core], own, load_sem)
    load.start()
    barrier = greet(z, dp, s, core)

    def greet_z(i, carry):
        @pl.when(i != z)
        def _():
            pl.semaphore_signal(
                barrier, inc=1, device_id=(2 * i + core, s), device_id_type=MESH
            )

        return carry

    lax.fori_loop(0, SEQ, greet_z, 0)
    pl.semaphore_wait(barrier, 2 * SEQ - 1 + SEQ - 1)

    def swap(t):
        return pltpu.make_async_remote_copy(
            src_ref=dkv_hbm.at[1 - core, t], dst_ref=mate.at[t],
            send_sem=pass_send.at[t], recv_sem=pass_recv.at[t],
            device_id=other, device_id_type=MESH,
        )

    def along(i):
        return pltpu.make_async_remote_copy(
            src_ref=gain_ref, dst_ref=along_z.at[z], send_sem=zs.at[i], recv_sem=zr.at[z],
            device_id=(2 * i + core, s), device_id_type=MESH,
        )

    def across(i):
        return pltpu.make_async_remote_copy(
            src_ref=z_sum, dst_ref=plane.at[core * SEQ + s],
            send_sem=ps.at[i], recv_sem=pr.at[core * SEQ + s],
            device_id=(2 * z + lax.div(i, SEQ), lax.rem(i, SEQ)), device_id_type=MESH,
        )

    def copies(kind, src, dst, t):
        peer_dp = 2 * z + span
        me = (peer_dp == dp) & (t == s)
        slot = slot_q if kind == 0 else slot_kv
        remote = pltpu.make_async_remote_copy(
            src_ref=src, dst_ref=dst, send_sem=send_sem.at[kind, t],
            recv_sem=recv_sem.at[kind, slot], device_id=(peer_dp, t), device_id_type=MESH,
        )
        local = pltpu.make_async_copy(src, dst, recv_sem.at[kind, slot])
        return me, remote, local

    def parts(t):
        return ((0, dq_hbm.at[t], dq_out.at[slot_q]), (1, mine.at[t], dkv_out.at[slot_kv]))

    def send(kind, src, dst, t):
        me, remote, local = copies(kind, src, dst, t)

        @pl.when(me)
        def _():
            local.start()

        @pl.when(jnp.logical_not(me))
        def _():
            remote.start()

    def first(i, carry):
        @pl.when(i != z)
        def _():
            along(i).start()

        swap(lax.rem(s + i, SEQ)).start()
        return carry

    lax.fori_loop(0, SEQ, first, 0)
    along_z[z] = gain_ref[...]

    def send_q(i, carry):
        t = lax.rem(s + i, SEQ)
        send(*parts(t)[0], t)
        return carry

    lax.fori_loop(0, SEQ, send_q, 0)
    load.wait()

    def send_kv(i, carry):
        t = lax.rem(s + i, SEQ)
        swap(t).wait_recv()
        mine[t] = (own[t].astype(F32) + mate[t].astype(F32)).astype(BF16)
        send(*parts(t)[1], t)
        return carry

    lax.fori_loop(0, SEQ, send_kv, 0)

    def arrive_z(i, carry):
        @pl.when(i != z)
        def _():
            pltpu.make_async_copy(along_z.at[i], along_z.at[i], zr.at[i]).wait()

        return carry

    lax.fori_loop(0, SEQ, arrive_z, 0)
    z_sum[...] = jnp.sum(along_z[...], axis=0)

    def spread(i, carry):
        @pl.when(i != core * SEQ + s)
        def _():
            across(i).start()

        return carry

    lax.fori_loop(0, 2 * SEQ, spread, 0)
    plane[core * SEQ + s] = z_sum[...]

    def arrive_plane(i, carry):
        @pl.when(i != core * SEQ + s)
        def _():
            pltpu.make_async_copy(plane.at[i], plane.at[i], pr.at[i]).wait()

        return carry

    lax.fori_loop(0, 2 * SEQ, arrive_plane, 0)
    gain_out[...] = jnp.sum(plane[...], axis=0)

    def finish(t, carry):
        pltpu.make_async_copy(dq_out.at[t], dq_out.at[t], recv_sem.at[0, t]).wait()
        pltpu.make_async_copy(dkv_out.at[t], dkv_out.at[t], recv_sem.at[1, t]).wait()
        swap(t).wait_send()

        @pl.when(t != z)
        def _():
            along(t).wait_send()

        for part in parts(t):
            me, remote, local = copies(*part, t)

            @pl.when(jnp.logical_not(me))
            def _():
                remote.wait_send()

        return carry

    lax.fori_loop(0, SEQ, finish, 0)

    def drain(i, carry):
        @pl.when(i != core * SEQ + s)
        def _():
            across(i).wait_send()

        return carry

    lax.fori_loop(0, 2 * SEQ, drain, 0)


def norm_kernel(
    where_ref, dq_ref, dkv_ref, q_ref, k_ref, qg_ref, kg_ref, gain_ref, near_ref, far_ref,
    gq_ref, gk_ref, gv_ref, gqg_ref, gkg_ref,
    q_wide, k_wide, v_wide,
):
    cosine, sine = block_rope(near_ref, far_ref, where_ref[0])
    q_wide[...] = q_ref[...].astype(F32).reshape(TOK * 16, HD)
    k_wide[...] = k_ref[...].astype(F32).reshape(TOK * 8, HD)

    def back(wide, rows_at, upstream, gain):
        rows = wide[rows_at, :]
        size = lax.rsqrt(jnp.mean(rows * rows, axis=1, keepdims=True) + EPS)
        unit = rows * size
        slope = turn_back(upstream.astype(F32), cosine, sine) * gain
        wide[rows_at, :] = size * (slope - unit * jnp.mean(slope * unit, axis=1, keepdims=True))

    def queries(h, carry):
        back(q_wide, pl.ds(h, TOK, stride=16), dq_ref[h], qg_ref[...])
        return carry

    def keys(j, carry):
        back(k_wide, pl.ds(j, TOK, stride=8), dkv_ref[j], kg_ref[...])
        v_wide[pl.ds(j, TOK, stride=8), :] = dkv_ref[8 + j].astype(F32)
        return carry

    lax.fori_loop(0, 16, queries, 0)
    gq_ref[...] = q_wide[...].reshape(TOK, 16, HD).astype(BF16)
    lax.fori_loop(0, 8, keys, 0)
    gk_ref[...] = k_wide[...].reshape(TOK, 8, HD).astype(BF16)
    gv_ref[...] = v_wide[...].reshape(TOK, 8, HD).astype(BF16)
    gqg_ref[...] = gain_ref[0:1, :] / (qg_ref[...] * QMUL)
    gkg_ref[...] = gain_ref[1:2, :] / kg_ref[...]


def shape(dims, dtype):
    return jax.ShapeDtypeStruct(dims, dtype)


def body(q_pre, k_pre, values, grad_out, segment_ids, q_gain, k_gain):
    near, far = (jnp.asarray(table) for table in rope_tables())
    qg, kg = q_gain.reshape(1, HD), k_gain.reshape(1, HD)
    dma = pltpu.SemaphoreType.DMA
    tiles = (SEQ, TOK, HD)
    q_all, g_all, kv_all, seg_all = pl.pallas_call(
        gather_kernel,
        name="gather_heads",
        out_shape=(
            shape(tiles, BF16), shape(tiles, BF16), shape((2,) + tiles, BF16),
            shape((SEQ, 1, TOK), jnp.int32),
        ),
        in_specs=[ANY] * 4 + [VM] * 5,
        out_specs=(ANY,) * 4,
        scratch_shapes=[
            pltpu.VMEM((TOK, 16, HD), BF16), pltpu.VMEM((TOK, 8, HD), BF16),
            pltpu.VMEM((TOK, 8, HD), BF16), pltpu.VMEM((TOK, 16, HD), BF16),
            pltpu.VMEM((TOK * 16, HD), F32), pltpu.VMEM((TOK * 8, HD), F32),
            pltpu.VMEM((TOK * 8, HD), F32), pltpu.VMEM((TOK * 16, HD), F32),
            pltpu.VMEM(tiles, BF16), pltpu.VMEM(tiles, BF16),
            pltpu.VMEM((2, 8, TOK, HD), BF16),
            dma((4,)), dma((4, SEQ)), dma((4, SEQ)), dma((SEQ,)), dma((SEQ,)),
        ],
        compiler_params=pltpu.CompilerParams(
            collective_id=0, has_side_effects=True, vmem_limit_bytes=32 << 20
        ),
    )(q_pre[0], k_pre[0], values[0], grad_out[0], segment_ids, qg, kg, near, far)

    dq, dkv, gains = pl.pallas_call(
        attend_kernel,
        name="attend_back",
        out_shape=(shape(tiles, BF16), shape((2,) + tiles, BF16), shape((8, HD), F32)),
        in_specs=[VM] * 6,
        out_specs=(VM,) * 3,
        scratch_shapes=[
            pltpu.VMEM((BAND, BLK, BLK), F32), pltpu.VMEM((BAND, BLK, BLK), F32),
            pltpu.VMEM((TOTAL, HD), F32), pltpu.VMEM((TOTAL, HD), F32),
            pltpu.VMEM((SEQ, TOK), jnp.int32), pltpu.VMEM((BLK, HD), F32),
        ],
        compiler_params=pltpu.CompilerParams(vmem_limit_bytes=40 << 20),
    )(q_all, g_all, kv_all, seg_all, near, far)

    dq_back, dkv_back, gain_sums = pl.pallas_call(
        scatter_kernel,
        name="return_tokens",
        out_shape=(shape(tiles, BF16), shape(tiles, BF16), shape((8, HD), F32)),
        in_specs=[ANY, ANY, VM],
        out_specs=(ANY, ANY, VM),
        scratch_shapes=[
            pltpu.VMEM(tiles, BF16), pltpu.VMEM(tiles, BF16), pltpu.VMEM(tiles, BF16),
            pltpu.VMEM((SEQ, 8, HD), F32), pltpu.VMEM((2 * SEQ, 8, HD), F32),
            pltpu.VMEM((8, HD), F32),
            dma, dma((2, SEQ)), dma((2, SEQ)), dma((SEQ,)), dma((SEQ,)),
            dma((SEQ,)), dma((SEQ,)), dma((2 * SEQ,)), dma((2 * SEQ,)),
        ],
        compiler_params=pltpu.CompilerParams(
            collective_id=1, has_side_effects=True, vmem_limit_bytes=32 << 20
        ),
    )(dq, dkv, gains)

    where = lax.axis_index("seq").astype(jnp.int32).reshape(1)
    grad_q, grad_k, grad_v, grad_qg, grad_kg = pl.pallas_call(
        norm_kernel,
        name="norm_back",
        out_shape=(
            shape((TOK, 16, HD), BF16), shape((TOK, 8, HD), BF16), shape((TOK, 8, HD), BF16),
            shape((1, HD), F32), shape((1, HD), F32),
        ),
        in_specs=[pl.BlockSpec(memory_space=pltpu.SMEM)] + [VM] * 9,
        out_specs=(VM,) * 5,
        scratch_shapes=[
            pltpu.VMEM((TOK * 16, HD), F32), pltpu.VMEM((TOK * 8, HD), F32),
            pltpu.VMEM((TOK * 8, HD), F32),
        ],
        compiler_params=pltpu.CompilerParams(vmem_limit_bytes=32 << 20),
    )(where, dq_back, dkv_back, q_pre[0], k_pre[0], qg, kg, gain_sums, near, far)
    return (
        grad_q[None], grad_k[None], grad_v[None], grad_qg.reshape(HD), grad_kg.reshape(HD)
    )


def solution(mesh):
    tokens = P("dp", "seq", None, None)
    return jax.shard_map(
        body,
        mesh=mesh,
        in_specs=(tokens, tokens, tokens, tokens, P("dp", "seq"), P(), P()),
        out_specs=(tokens, tokens, tokens, P(), P()),
        check_vma=False,
    )
```

```python
import jax
import jax.numpy as jnp
import numpy as np
from jax import lax
from jax.experimental import pallas as pl
from jax.experimental.pallas import tpu as pltpu
from jax.sharding import PartitionSpec as P

PRESCALE = 168
HD = 128
SEQ = 16
TOK = 128
TOTAL = SEQ * TOK
BLK = 256
NBLK = TOTAL // BLK
BAND = 5
EPS = 1e-6
ROPE_BASE = 1000000.0
ROPE_FACTOR = 8.0
SCALE = float(PRESCALE) ** (-0.5)
QMUL = SCALE * float(np.log2(np.e))
LN2 = float(np.log(2.0))
MESH = pl.DeviceIdType.MESH
F32 = jnp.float32
BF16 = jnp.bfloat16
ANY = pl.BlockSpec(memory_space=pl.ANY)
HBM = pl.BlockSpec(memory_space=pltpu.HBM)
VM = pl.BlockSpec(memory_space=pltpu.VMEM)


def rope_tables():
    half = HD // 2
    freqs = ROPE_BASE ** (-(np.arange(half, dtype=np.float64) * 2.0 / HD))
    freqs = np.concatenate([freqs, freqs])
    near = np.arange(TOK, dtype=np.float64)[:, None] / ROPE_FACTOR * freqs[None, :]
    far = np.arange(SEQ, dtype=np.float64)[:, None] * TOK / ROPE_FACTOR * freqs[None, :]
    return (
        np.stack([np.cos(near), np.sin(near)]).astype(np.float32),
        np.stack([np.cos(far), np.sin(far)], axis=1).astype(np.float32),
    )


def block_rope(near_ref, far_ref, block):
    far = far_ref[block]
    cb, sb = far[0:1, :], far[1:2, :]
    cosine = near_ref[0] * cb - near_ref[1] * sb
    sine = near_ref[1] * cb + near_ref[0] * sb
    lane = lax.broadcasted_iota(jnp.int32, (TOK, HD), 1)
    return cosine, jnp.where(lane < HD // 2, -sine, sine)


def turn(rows, cosine, sine):
    return rows * cosine + pltpu.roll(rows, HD // 2, 1) * sine


def turn_back(rows, cosine, sine):
    return rows * cosine - pltpu.roll(rows, HD // 2, 1) * sine


def place():
    dp = lax.axis_index("dp")
    s = lax.axis_index("seq")
    z = lax.div(dp, 2)
    return dp, s, z, lax.rem(dp, 2)


def fused_kernel(
    q_hbm, k_hbm, v_hbm, g_hbm, seg_hbm, qg_hbm, kg_hbm, near_hbm, far_hbm,
    dq_out, dkv_out, gain_out,
    q_raw, k_raw, v_raw, g_raw, seg_one, qg_ref, kg_ref, near_ref, far_ref,
    q_wide, k_wide, v_wide, g_wide, q_buf, g_buf, kv_buf,
    q_all, g_all, kv_all, seg_all, first_ref, inv_ref,
    expo, pgrad, dq_acc, dk_acc, dv_acc, gain_acc,
    dq_buf, dkv_buf, mate, mine, gain_one, along_z, plane, z_sum,
    load_sem, send_sem, recv_sem, pass_send, pass_recv,
    back_send, back_recv, swap_send, swap_recv, zs, zr, ps, pr,
):
    dp, s, z, core = place()
    j_own = lax.div(s, 2)
    span = lax.rem(s, 2)
    mate_at = (2 * z + 1 - core, s)
    loads = [
        pltpu.make_async_copy(src, dst, load_sem.at[i])
        for i, (src, dst) in enumerate(
            (
                (k_hbm, k_raw), (near_hbm, near_ref), (far_hbm, far_ref), (kg_hbm, kg_ref),
                (qg_hbm, qg_ref), (seg_hbm, seg_one), (q_hbm, q_raw), (v_hbm, v_raw),
                (g_hbm, g_raw),
            )
        )
    ]
    for copy in loads:
        copy.start()
    barrier = pltpu.get_barrier_semaphore()

    def greet(i, carry):
        @pl.when(i != core * SEQ + s)
        def _():
            pl.semaphore_signal(
                barrier, inc=1, device_id=(2 * z + lax.div(i, SEQ), lax.rem(i, SEQ)),
                device_id_type=MESH,
            )

        return carry

    def greet_z(i, carry):
        @pl.when(i != z)
        def _():
            pl.semaphore_signal(
                barrier, inc=1, device_id=(2 * i + core, s), device_id_type=MESH
            )

        return carry

    lax.fori_loop(0, 2 * SEQ, greet, 0)
    lax.fori_loop(0, SEQ, greet_z, 0)
    for copy in loads[:6]:
        copy.wait()
    cosine, sine = block_rope(near_ref, far_ref, s)
    k_wide[...] = k_raw[...].astype(F32).reshape(TOK * 8, HD)
    pl.semaphore_wait(barrier, 2 * SEQ - 1 + SEQ - 1)

    def is_me(j, r):
        return (2 * z + r == dp) & (2 * j + core == s)

    def outward(kind, src, dst, j, r):
        return pltpu.make_async_remote_copy(
            src_ref=src, dst_ref=dst, send_sem=send_sem.at[kind, 2 * j + r],
            recv_sem=recv_sem.at[kind, s], device_id=(2 * z + r, 2 * j + core),
            device_id_type=MESH,
        )

    def send(part, j, r):
        kind, src, dst = part
        me = is_me(j, r)

        @pl.when(me)
        def _():
            pltpu.make_async_copy(src, dst, recv_sem.at[kind, s]).start()

        @pl.when(jnp.logical_not(me))
        def _():
            outward(kind, src, dst, j, r).start()

    def part_of(kind, j, r):
        h = 2 * j + r
        if kind == 0:
            return (0, g_buf.at[h], g_all.at[s])
        if kind == 1:
            return (1, kv_buf.at[r, j], kv_all.at[r, s])
        if kind == 2:
            return (2, q_buf.at[h], q_all.at[s])
        return (3, seg_one, seg_all.at[s])

    def turns(t):
        return lax.rem(j_own + t, SEQ // 2)

    def send_k(t, carry):
        j = turns(t)
        rows = k_wide[pl.ds(j, TOK, stride=8), :]
        size = lax.rsqrt(jnp.mean(rows * rows, axis=1, keepdims=True) + EPS)
        kv_buf[0, j] = turn(rows * size * kg_ref[...], cosine, sine).astype(BF16)
        send(part_of(1, j, 0), j, 0)
        for r in range(2):
            send(part_of(3, j, r), j, r)
        return carry

    lax.fori_loop(0, 8, send_k, 0)
    loads[6].wait()
    q_wide[...] = q_raw[...].astype(F32).reshape(TOK * 16, HD)

    def send_q(t, carry):
        j = turns(t)
        for r in range(2):
            h = 2 * j + r
            rows = q_wide[pl.ds(h, TOK, stride=16), :]
            size = lax.rsqrt(jnp.mean(rows * rows, axis=1, keepdims=True) + EPS)
            q_buf[h] = (turn(rows * size * qg_ref[...], cosine, sine) * QMUL).astype(BF16)
            send(part_of(2, j, r), j, r)
        return carry

    lax.fori_loop(0, 8, send_q, 0)
    loads[7].wait()
    v_wide[...] = v_raw[...].astype(F32).reshape(TOK * 8, HD)

    def send_v(t, carry):
        j = turns(t)
        kv_buf[1, j] = v_wide[pl.ds(j, TOK, stride=8), :].astype(BF16)
        send(part_of(1, j, 1), j, 1)
        return carry

    lax.fori_loop(0, 8, send_v, 0)
    loads[8].wait()
    g_wide[...] = g_raw[...].astype(F32).reshape(TOK * 16, HD)

    def send_g(t, carry):
        j = turns(t)
        for r in range(2):
            h = 2 * j + r
            g_buf[h] = g_wide[pl.ds(h, TOK, stride=16), :].astype(BF16)
            send(part_of(0, j, r), j, r)
        return carry

    lax.fori_loop(0, 8, send_g, 0)

    def passing(kind, t):
        return pltpu.make_async_remote_copy(
            src_ref=kv_all.at[kind, t], dst_ref=kv_all.at[kind, t],
            send_sem=pass_send.at[t], recv_sem=pass_recv.at[t],
            device_id=mate_at, device_id_type=MESH,
        )

    def arrive(kind, t, ref):
        pltpu.make_async_copy(ref, ref, recv_sem.at[kind, t]).wait()

    def forward(i, carry):
        t = lax.rem(s + i, SEQ)
        arrive(1, t, kv_all.at[core, t])
        passing(core, t).start()
        return carry

    @pl.when(core == 0)
    def _():
        lax.fori_loop(0, SEQ, forward, 0)

    def got_first(t, carry):
        arrive(2, t, q_all.at[t])
        arrive(3, t, seg_all.at[t])

        @pl.when(core == 1)
        def _():
            passing(0, t).wait_recv()

        return carry

    lax.fori_loop(0, SEQ, got_first, 0)

    seg = seg_all[...].reshape(SEQ, TOK)
    first = jnp.zeros((SEQ, TOK), F32)
    for d in range(1, 8):
        below = jnp.where(seg < d, 1.0, 0.0)
        count = jnp.sum(jnp.sum(below, axis=1, keepdims=True), axis=0, keepdims=True)
        first = jnp.where(seg == d, count, first)
    first_ref[...] = first.astype(jnp.int32).reshape(SEQ, 1, TOK)
    dk_acc[...] = jnp.zeros_like(dk_acc)
    dv_acc[...] = jnp.zeros_like(dv_acc)
    gain_acc[...] = jnp.zeros_like(gain_acc)
    last = (((1,), (1,)), ((), ()))
    lead = (((0,), (0,)), ((), ()))

    def pair(ref, qi):
        return ref[pl.ds(2 * qi, 2)].reshape(BLK, HD)

    def keys_of(kind, kb):
        return kv_all[kind, pl.ds(2 * kb, 2)].reshape(BLK, HD)

    def fold(x):
        return jnp.sum(x.reshape(BLK // 8, 8, BLK), axis=0)

    def forward_block(i, carry):
        qi = turns(i)
        queries = pair(q_all, qi)
        firsts = jnp.concatenate([first_ref[2 * qi], first_ref[2 * qi + 1]], axis=1)
        key_at = lax.broadcasted_iota(jnp.int32, (BLK, BLK), 0)
        query_at = lax.broadcasted_iota(jnp.int32, (BLK, BLK), 1)
        total = jnp.zeros((8, BLK), F32)
        for d in range(BAND):
            kb = jnp.maximum(qi - d, 0)
            st = lax.dot_general(keys_of(0, kb), queries, last, preferred_element_type=F32)
            seen = key_at >= firsts - (qi - d) * BLK
            if d == 0:
                seen = seen & (key_at <= query_at)
            e = jnp.where(seen, jnp.exp2(st), 0.0)
            expo[qi, d] = e
            total = total + fold(e)
        inv_ref[qi] = 1.0 / jnp.sum(total, axis=0, keepdims=True)
        return carry

    lax.fori_loop(0, NBLK, forward_block, 0)

    @pl.when(core == 1)
    def _():
        lax.fori_loop(0, SEQ, forward, 0)

    def got_second(t, carry):
        arrive(0, t, g_all.at[t])

        @pl.when(core == 0)
        def _():
            passing(1, t).wait_recv()

        return carry

    lax.fori_loop(0, SEQ, got_second, 0)

    slot_q = 2 * j_own + core
    slot_kv = core * 8 + j_own

    def homeward(kind, src, dst, t):
        return pltpu.make_async_remote_copy(
            src_ref=src, dst_ref=dst, send_sem=back_send.at[kind, t],
            recv_sem=back_recv.at[kind, slot_q if kind == 0 else slot_kv],
            device_id=(2 * z + span, t), device_id_type=MESH,
        )

    def back_part(kind, t):
        if kind == 0:
            return (0, dq_buf.at[t], dq_out.at[slot_q])
        return (1, mine.at[t], dkv_out.at[slot_kv])

    def home(t):
        return (span == core) & (t == s)

    def send_back(part, t):
        kind, src, dst = part

        @pl.when(home(t))
        def _():
            pltpu.make_async_copy(
                src, dst, back_recv.at[kind, slot_q if kind == 0 else slot_kv]
            ).start()

        @pl.when(jnp.logical_not(home(t)))
        def _():
            homeward(kind, src, dst, t).start()

    def backward_block(i, carry):
        qi = turns(i)
        queries = pair(q_all, qi)
        upstream = pair(g_all, qi)
        inv = inv_ref[qi]
        mixed = jnp.zeros((8, BLK), F32)
        for d in range(BAND):
            kb = jnp.maximum(qi - d, 0)
            dpt = lax.dot_general(keys_of(1, kb), upstream, last, preferred_element_type=F32)
            pgrad[d] = dpt
            mixed = mixed + fold(expo[qi, d] * dpt)
        delta = jnp.sum(mixed, axis=0, keepdims=True) * inv
        dq = jnp.zeros((BLK, HD), F32)
        for d in range(BAND):
            kb = jnp.maximum(qi - d, 0)
            p = expo[qi, d] * inv
            ds = (p * (pgrad[d] - delta)).astype(BF16)
            p = p.astype(BF16)
            rows = pl.ds(pl.multiple_of(kb * BLK, BLK), BLK)
            dv_acc[rows, :] += jnp.dot(p, upstream, preferred_element_type=F32)
            dk_acc[rows, :] += jnp.dot(ds, queries, preferred_element_type=F32)
            dq = dq + lax.dot_general(ds, keys_of(0, kb), lead, preferred_element_type=F32)
        dq = dq * SCALE
        gain = gain_acc[...]
        for half in range(2):
            block = 2 * qi + half
            rows = dq[half * TOK:(half + 1) * TOK, :]
            dq_buf[block] = rows.astype(BF16)
            send_back(back_part(0, block), block)
            cb, sb = block_rope(near_ref, far_ref, block)
            both = turn_back(rows, cb, sb) * turn_back(q_all[block].astype(F32), cb, sb)
            gain = gain + jnp.sum(both.reshape(TOK // 8, 8, HD), axis=0)
        gain_acc[...] = gain
        return carry

    lax.fori_loop(0, NBLK, backward_block, 0)

    def swap(t):
        return pltpu.make_async_remote_copy(
            src_ref=dkv_buf.at[1 - core, t], dst_ref=mate.at[t],
            send_sem=swap_send.at[t], recv_sem=swap_recv.at[t],
            device_id=mate_at, device_id_type=MESH,
        )

    def keys_out(i, gain_k):
        block = lax.rem(s + i, SEQ)
        rows = pl.ds(pl.multiple_of(block * TOK, TOK), TOK)
        dk = dk_acc[rows, :] * LN2
        dkv_buf[0, block] = dk.astype(BF16)
        dkv_buf[1, block] = dv_acc[rows, :].astype(BF16)
        swap(block).start()
        cb, sb = block_rope(near_ref, far_ref, block)
        both = turn_back(dk, cb, sb) * turn_back(kv_all[0, block].astype(F32), cb, sb)
        return gain_k + jnp.sum(both.reshape(TOK // 8, 8, HD), axis=0)

    gain_k = lax.fori_loop(0, SEQ, keys_out, jnp.zeros((8, HD), F32))
    row = lax.broadcasted_iota(jnp.int32, (8, HD), 0)
    gain_one[...] = jnp.where(
        row == 0,
        jnp.sum(gain_acc[...], axis=0, keepdims=True),
        jnp.where(row == 1, jnp.sum(gain_k, axis=0, keepdims=True), 0.0),
    )

    def along(i):
        return pltpu.make_async_remote_copy(
            src_ref=gain_one, dst_ref=along_z.at[z], send_sem=zs.at[i], recv_sem=zr.at[z],
            device_id=(2 * i + core, s), device_id_type=MESH,
        )

    def across(i):
        return pltpu.make_async_remote_copy(
            src_ref=z_sum, dst_ref=plane.at[core * SEQ + s],
            send_sem=ps.at[i], recv_sem=pr.at[core * SEQ + s],
            device_id=(2 * z + lax.div(i, SEQ), lax.rem(i, SEQ)), device_id_type=MESH,
        )

    def gains_off(i, carry):
        @pl.when(i != z)
        def _():
            along(i).start()

        return carry

    lax.fori_loop(0, SEQ, gains_off, 0)
    along_z[z] = gain_one[...]

    def send_kv(i, carry):
        t = lax.rem(s + i, SEQ)
        swap(t).wait_recv()
        mine[t] = (dkv_buf[core, t].astype(F32) + mate[t].astype(F32)).astype(BF16)
        send_back(back_part(1, t), t)
        return carry

    lax.fori_loop(0, SEQ, send_kv, 0)

    def arrive_z(i, carry):
        @pl.when(i != z)
        def _():
            pltpu.make_async_copy(along_z.at[i], along_z.at[i], zr.at[i]).wait()

        return carry

    lax.fori_loop(0, SEQ, arrive_z, 0)
    z_sum[...] = jnp.sum(along_z[...], axis=0)

    def spread(i, carry):
        @pl.when(i != core * SEQ + s)
        def _():
            across(i).start()

        return carry

    lax.fori_loop(0, 2 * SEQ, spread, 0)
    plane[core * SEQ + s] = z_sum[...]

    def drain(j, carry):
        for r in range(2):
            for kind in (0, 2, 3):
                @pl.when(jnp.logical_not(is_me(j, r)))
                def _(kind=kind, r=r):
                    outward(*part_of(kind, j, r), j, r).wait_send()

            @pl.when(jnp.logical_not(is_me(j, r)))
            def _(r=r):
                outward(*part_of(1, j, r), j, r).wait_send()

        return carry

    lax.fori_loop(0, 8, drain, 0)

    def drain_back(t, carry):
        passing(core, t).wait_send()
        swap(t).wait_send()

        @pl.when(t != z)
        def _():
            along(t).wait_send()

        for kind in range(2):
            @pl.when(jnp.logical_not(home(t)))
            def _(kind=kind):
                homeward(*back_part(kind, t), t).wait_send()

        return carry

    lax.fori_loop(0, SEQ, drain_back, 0)

    def arrive_plane(i, carry):
        @pl.when(i != core * SEQ + s)
        def _():
            pltpu.make_async_copy(plane.at[i], plane.at[i], pr.at[i]).wait()
            across(i).wait_send()

        return carry

    lax.fori_loop(0, 2 * SEQ, arrive_plane, 0)
    gain_out[...] = jnp.sum(plane[...], axis=0)

    def arrive_back(t, carry):
        pltpu.make_async_copy(dq_out.at[t], dq_out.at[t], back_recv.at[0, t]).wait()
        pltpu.make_async_copy(dkv_out.at[t], dkv_out.at[t], back_recv.at[1, t]).wait()
        return carry

    lax.fori_loop(0, SEQ, arrive_back, 0)


def norm_kernel(
    where_ref, dq_ref, dkv_ref, q_ref, k_ref, qg_ref, kg_ref, gain_ref, near_ref, far_ref,
    gq_ref, gk_ref, gv_ref, gqg_ref, gkg_ref,
    q_wide, k_wide, q_new, k_new, v_new,
):
    cosine, sine = block_rope(near_ref, far_ref, where_ref[0])
    q_wide[...] = q_ref[...].astype(F32).reshape(TOK * 16, HD)
    k_wide[...] = k_ref[...].astype(F32).reshape(TOK * 8, HD)

    def back(wide, new, rows_at, upstream, gain):
        rows = wide[rows_at, :]
        size = lax.rsqrt(jnp.mean(rows * rows, axis=1, keepdims=True) + EPS)
        unit = rows * size
        slope = turn_back(upstream.astype(F32), cosine, sine) * gain
        new[rows_at, :] = size * (slope - unit * jnp.mean(slope * unit, axis=1, keepdims=True))

    for h in range(16):
        back(q_wide, q_new, pl.ds(h, TOK, stride=16), dq_ref[h], qg_ref[...])
    for j in range(8):
        back(k_wide, k_new, pl.ds(j, TOK, stride=8), dkv_ref[j], kg_ref[...])
        v_new[pl.ds(j, TOK, stride=8), :] = dkv_ref[8 + j].astype(F32)
    gq_ref[...] = q_new[...].reshape(TOK, 16, HD).astype(BF16)
    gk_ref[...] = k_new[...].reshape(TOK, 8, HD).astype(BF16)
    gv_ref[...] = v_new[...].reshape(TOK, 8, HD).astype(BF16)
    gqg_ref[...] = gain_ref[0:1, :] / (qg_ref[...] * QMUL)
    gkg_ref[...] = gain_ref[1:2, :] / kg_ref[...]


def shape(dims, dtype):
    return jax.ShapeDtypeStruct(dims, dtype)


def body(q_pre, k_pre, values, grad_out, segment_ids, q_gain, k_gain):
    near, far = (jnp.asarray(table) for table in rope_tables())
    qg, kg = q_gain.reshape(1, HD), k_gain.reshape(1, HD)
    dma = pltpu.SemaphoreType.DMA
    tiles = (SEQ, TOK, HD)
    dq_back, dkv_back, gain_sums = pl.pallas_call(
        fused_kernel,
        name="heads_and_back",
        out_shape=(shape(tiles, BF16), shape(tiles, BF16), shape((8, HD), F32)),
        in_specs=[HBM] * 9,
        out_specs=(ANY, ANY, VM),
        scratch_shapes=[
            pltpu.VMEM((TOK, 16, HD), BF16), pltpu.VMEM((TOK, 8, HD), BF16),
            pltpu.VMEM((TOK, 8, HD), BF16), pltpu.VMEM((TOK, 16, HD), BF16),
            pltpu.VMEM((1, TOK), jnp.int32), pltpu.VMEM((1, HD), F32), pltpu.VMEM((1, HD), F32),
            pltpu.VMEM((2, TOK, HD), F32), pltpu.VMEM((SEQ, 2, HD), F32),
            pltpu.VMEM((TOK * 16, HD), F32), pltpu.VMEM((TOK * 8, HD), F32),
            pltpu.VMEM((TOK * 8, HD), F32), pltpu.VMEM((TOK * 16, HD), F32),
            pltpu.VMEM(tiles, BF16), pltpu.VMEM(tiles, BF16),
            pltpu.VMEM((2, 8, TOK, HD), BF16),
            pltpu.VMEM(tiles, BF16), pltpu.VMEM(tiles, BF16), pltpu.VMEM((2,) + tiles, BF16),
            pltpu.VMEM((SEQ, 1, TOK), jnp.int32), pltpu.VMEM((SEQ, 1, TOK), jnp.int32),
            pltpu.VMEM((NBLK, 1, BLK), F32),
            pltpu.VMEM((NBLK, BAND, BLK, BLK), F32), pltpu.VMEM((BAND, BLK, BLK), F32),
            pltpu.VMEM((BLK, HD), F32), pltpu.VMEM((TOTAL, HD), F32),
            pltpu.VMEM((TOTAL, HD), F32), pltpu.VMEM((8, HD), F32),
            pltpu.VMEM(tiles, BF16), pltpu.VMEM((2,) + tiles, BF16),
            pltpu.VMEM(tiles, BF16), pltpu.VMEM(tiles, BF16),
            pltpu.VMEM((8, HD), F32), pltpu.VMEM((SEQ, 8, HD), F32),
            pltpu.VMEM((2 * SEQ, 8, HD), F32), pltpu.VMEM((8, HD), F32),
            dma((9,)), dma((4, SEQ)), dma((4, SEQ)), dma((SEQ,)), dma((SEQ,)),
            dma((2, SEQ)), dma((2, SEQ)), dma((SEQ,)), dma((SEQ,)),
            dma((SEQ,)), dma((SEQ,)), dma((2 * SEQ,)), dma((2 * SEQ,)),
        ],
        compiler_params=pltpu.CompilerParams(
            collective_id=0, has_side_effects=True, vmem_limit_bytes=48 << 20
        ),
    )(q_pre[0], k_pre[0], values[0], grad_out[0], segment_ids, qg, kg, near, far)

    where = lax.axis_index("seq").astype(jnp.int32).reshape(1)
    grad_q, grad_k, grad_v, grad_qg, grad_kg = pl.pallas_call(
        norm_kernel,
        name="norm_back",
        out_shape=(
            shape((TOK, 16, HD), BF16), shape((TOK, 8, HD), BF16), shape((TOK, 8, HD), BF16),
            shape((1, HD), F32), shape((1, HD), F32),
        ),
        in_specs=[pl.BlockSpec(memory_space=pltpu.SMEM)] + [VM] * 9,
        out_specs=(VM,) * 5,
        scratch_shapes=[
            pltpu.VMEM((TOK * 16, HD), F32), pltpu.VMEM((TOK * 8, HD), F32),
            pltpu.VMEM((TOK * 16, HD), F32), pltpu.VMEM((TOK * 8, HD), F32),
            pltpu.VMEM((TOK * 8, HD), F32),
        ],
        compiler_params=pltpu.CompilerParams(vmem_limit_bytes=32 << 20),
    )(where, dq_back, dkv_back, q_pre[0], k_pre[0], qg, kg, gain_sums, near, far)
    return (
        grad_q[None], grad_k[None], grad_v[None], grad_qg.reshape(HD), grad_kg.reshape(HD)
    )


def solution(mesh):
    tokens = P("dp", "seq", None, None)
    return jax.shard_map(
        body,
        mesh=mesh,
        in_specs=(tokens, tokens, tokens, tokens, P("dp", "seq"), P(), P()),
        out_specs=(tokens, tokens, tokens, P(), P()),
        check_vma=False,
    )
```

```python
import jax
import jax.numpy as jnp
import numpy as np
from jax import lax
from jax.experimental import pallas as pl
from jax.experimental.pallas import tpu as pltpu
from jax.sharding import PartitionSpec as P

PRESCALE = 168
HD = 128
SEQ = 16
TOK = 128
TOTAL = SEQ * TOK
BLK = 256
NBLK = TOTAL // BLK
BAND = 5
EPS = 1e-6
ROPE_BASE = 1000000.0
ROPE_FACTOR = 8.0
SCALE = float(PRESCALE) ** (-0.5)
QMUL = SCALE * float(np.log2(np.e))
LN2 = float(np.log(2.0))
MESH = pl.DeviceIdType.MESH
F32 = jnp.float32
BF16 = jnp.bfloat16
ANY = pl.BlockSpec(memory_space=pl.ANY)
HBM = pl.BlockSpec(memory_space=pltpu.HBM)
VM = pl.BlockSpec(memory_space=pltpu.VMEM)


def rope_tables():
    half = HD // 2
    freqs = ROPE_BASE ** (-(np.arange(half, dtype=np.float64) * 2.0 / HD))
    freqs = np.concatenate([freqs, freqs])
    near = np.arange(TOK, dtype=np.float64)[:, None] / ROPE_FACTOR * freqs[None, :]
    far = np.arange(SEQ, dtype=np.float64)[:, None] * TOK / ROPE_FACTOR * freqs[None, :]
    return (
        np.stack([np.cos(near), np.sin(near)]).astype(np.float32),
        np.stack([np.cos(far), np.sin(far)], axis=1).astype(np.float32),
    )


def block_rope(near_ref, far_ref, block):
    far = far_ref[block]
    cb, sb = far[0:1, :], far[1:2, :]
    cosine = near_ref[0] * cb - near_ref[1] * sb
    sine = near_ref[1] * cb + near_ref[0] * sb
    lane = lax.broadcasted_iota(jnp.int32, (TOK, HD), 1)
    return cosine, jnp.where(lane < HD // 2, -sine, sine)


def turn(rows, cosine, sine):
    return rows * cosine + pltpu.roll(rows, HD // 2, 1) * sine


def turn_back(rows, cosine, sine):
    return rows * cosine - pltpu.roll(rows, HD // 2, 1) * sine


def place():
    dp = lax.axis_index("dp")
    s = lax.axis_index("seq")
    z = lax.div(dp, 2)
    return dp, s, z, lax.rem(dp, 2)


def fused_kernel(
    q_hbm, k_hbm, v_hbm, g_hbm, seg_hbm, qg_hbm, kg_hbm, near_hbm, far_hbm,
    dq_out, dkv_out, gain_out,
    q_raw, k_raw, v_raw, g_raw, seg_one, qg_ref, kg_ref, near_ref, far_ref,
    q_wide, k_wide, v_wide, g_wide, q_buf, g_buf, kv_buf,
    q_all, g_all, kv_all, seg_all, first_ref, cos_all, sin_all, q_unit, k_unit,
    expo, prob, pgrad, dq_acc, gain_acc,
    dq_buf, dkv_buf, mate, mine, gain_one, stages,
    load_sem, send_sem, recv_sem, pass_send, pass_recv, pass_got,
    back_send, back_recv, swap_send, swap_recv, stage_send, stage_recv,
):
    dp, s, z, core = place()
    j_own = lax.div(s, 2)
    span = lax.rem(s, 2)
    mate_at = (2 * z + 1 - core, s)
    loads = [
        pltpu.make_async_copy(src, dst, load_sem.at[i])
        for i, (src, dst) in enumerate(
            (
                (k_hbm, k_raw), (near_hbm, near_ref), (far_hbm, far_ref), (kg_hbm, kg_ref),
                (qg_hbm, qg_ref), (seg_hbm, seg_one), (q_hbm, q_raw), (v_hbm, v_raw),
                (g_hbm, g_raw),
            )
        )
    ]
    for copy in loads:
        copy.start()
    barrier = pltpu.get_barrier_semaphore()

    def greet(i, carry):
        @pl.when(i != core * SEQ + s)
        def _():
            pl.semaphore_signal(
                barrier, inc=1, device_id=(2 * z + lax.div(i, SEQ), lax.rem(i, SEQ)),
                device_id_type=MESH,
            )

        return carry

    x_at, y_at = lax.rem(s, 4), lax.div(s, 4)
    z_low, z_high = lax.rem(z, 2), lax.div(z, 2)

    def member(stage, i):
        if stage == 0:
            return (2 * z + lax.rem(i, 2), 4 * y_at + lax.div(i, 2))
        if stage == 1:
            return (2 * (2 * z_high + lax.rem(i, 2)) + core, 4 * lax.div(i, 2) + x_at)
        return (2 * (2 * i + z_low) + core, s)

    rank = (2 * x_at + core, 2 * y_at + z_low, z_high)

    def greet_low(i, carry):
        pl.semaphore_signal(
            barrier, inc=1, device_id=member(1, 2 * i + 1 - z_low), device_id_type=MESH
        )
        return carry

    def greet_high(i, carry):
        @pl.when(i != z_high)
        def _():
            pl.semaphore_signal(barrier, inc=1, device_id=member(2, i), device_id_type=MESH)

        return carry

    lax.fori_loop(0, 2 * SEQ, greet, 0)
    lax.fori_loop(0, 4, greet_low, 0)
    lax.fori_loop(0, 8, greet_high, 0)
    for copy in loads[:6]:
        copy.wait()
    cosine, sine = block_rope(near_ref, far_ref, s)
    k_wide[...] = k_raw[...].astype(F32).reshape(TOK * 8, HD)
    pl.semaphore_wait(barrier, 2 * SEQ - 1 + 4 + 7)

    def is_me(j, r):
        return (2 * z + r == dp) & (2 * j + core == s)

    def landing(kind):
        return recv_sem.at[kind] if kind != 1 else pass_got.at[s]

    def outward(kind, src, dst, j, r):
        return pltpu.make_async_remote_copy(
            src_ref=src, dst_ref=dst, send_sem=send_sem.at[kind], recv_sem=landing(kind),
            device_id=(2 * z + r, 2 * j + core), device_id_type=MESH,
        )

    def send(part, j, r):
        kind, src, dst = part
        me = is_me(j, r)

        @pl.when(me)
        def _():
            pltpu.make_async_copy(src, dst, landing(kind)).start()

        @pl.when(jnp.logical_not(me))
        def _():
            outward(kind, src, dst, j, r).start()

    def part_of(kind, j, r):
        h = 2 * j + r
        if kind == 0:
            return (0, g_buf.at[h], g_all.at[s])
        if kind == 1:
            return (1, kv_buf.at[r, j], kv_all.at[r, s])
        if kind == 2:
            return (2, q_buf.at[h], q_all.at[s])
        return (3, seg_one, seg_all.at[s])

    def turns(t):
        return lax.rem(j_own + t, SEQ // 2)

    def send_k(t, carry):
        j = turns(t)
        rows = k_wide[pl.ds(j, TOK, stride=8), :]
        size = lax.rsqrt(jnp.mean(rows * rows, axis=1, keepdims=True) + EPS)
        kv_buf[0, j] = turn(rows * size * kg_ref[...], cosine, sine).astype(BF16)
        send(part_of(1, j, 0), j, 0)
        for r in range(2):
            send(part_of(3, j, r), j, r)
        return carry

    lax.fori_loop(0, 8, send_k, 0)
    loads[6].wait()
    q_wide[...] = q_raw[...].astype(F32).reshape(TOK * 16, HD)

    def send_q(t, carry):
        j = turns(t)
        for r in range(2):
            h = 2 * j + r
            rows = q_wide[pl.ds(h, TOK, stride=16), :]
            size = lax.rsqrt(jnp.mean(rows * rows, axis=1, keepdims=True) + EPS)
            q_buf[h] = (turn(rows * size * qg_ref[...], cosine, sine) * QMUL).astype(BF16)
            send(part_of(2, j, r), j, r)
        return carry

    lax.fori_loop(0, 8, send_q, 0)
    loads[8].wait()
    g_wide[...] = g_raw[...].astype(F32).reshape(TOK * 16, HD)

    def send_g(t, carry):
        j = turns(t)
        for r in range(2):
            h = 2 * j + r
            g_buf[h] = g_wide[pl.ds(h, TOK, stride=16), :].astype(BF16)
            send(part_of(0, j, r), j, r)
        return carry

    lax.fori_loop(0, 8, send_g, 0)

    loads[7].wait()
    v_wide[...] = v_raw[...].astype(F32).reshape(TOK * 8, HD)

    def send_v(t, carry):
        j = turns(t)
        kv_buf[1, j] = v_wide[pl.ds(j, TOK, stride=8), :].astype(BF16)
        send(part_of(1, j, 1), j, 1)
        return carry

    lax.fori_loop(0, 8, send_v, 0)
    def passing(kind, t):
        return pltpu.make_async_remote_copy(
            src_ref=kv_all.at[kind, t], dst_ref=kv_all.at[kind, t],
            send_sem=pass_send, recv_sem=pass_recv,
            device_id=mate_at, device_id_type=MESH,
        )

    def wait_on(ref, sem):
        pltpu.make_async_copy(ref, ref, sem).wait()

    def forward(i, carry):
        t = lax.rem(s + i, SEQ)
        wait_on(kv_all.at[core, t], pass_got.at[t])
        passing(core, t).start()
        return carry

    def tables(t, carry):
        cb, sb = block_rope(near_ref, far_ref, t)
        cos_all[t] = cb
        sin_all[t] = sb
        return carry

    lax.fori_loop(0, SEQ, tables, 0)

    @pl.when(core == 0)
    def _():
        lax.fori_loop(0, SEQ, forward, 0)

    wait_on(q_all, recv_sem.at[2])
    wait_on(seg_all, recv_sem.at[3])

    @pl.when(core == 1)
    def _():
        wait_on(kv_all.at[0], pass_recv)

    seg = seg_all[...].reshape(SEQ, TOK)
    first = jnp.zeros((SEQ, TOK), F32)
    for d in range(1, 8):
        below = jnp.where(seg < d, 1.0, 0.0)
        count = jnp.sum(jnp.sum(below, axis=1, keepdims=True), axis=0, keepdims=True)
        first = jnp.where(seg == d, count, first)
    first_ref[...] = first.astype(jnp.int32).reshape(SEQ, 1, TOK)
    gain_acc[...] = jnp.zeros_like(gain_acc)
    last = (((1,), (1,)), ((), ()))
    lead = (((0,), (0,)), ((), ()))

    def pair(ref, qi):
        return ref[pl.ds(2 * qi, 2)].reshape(BLK, HD)

    def keys_of(kind, kb):
        return kv_all[kind, pl.ds(2 * kb, 2)].reshape(BLK, HD)

    def fold(x):
        return jnp.sum(x.reshape(BLK // 8, 8, BLK), axis=0)

    def by_queries(i, run):
        qi = turns(i)
        for count in range(1, BAND + 1):
            fits = (qi >= BAND - 1) if count == BAND else (qi == count - 1)

            @pl.when(fits)
            def _(count=count):
                run(qi, count)

    def by_keys(i, run):
        kb = turns(i)
        for count in range(1, BAND + 1):
            fits = (kb <= NBLK - BAND) if count == BAND else (kb == NBLK - count)

            @pl.when(fits)
            def _(count=count):
                run(kb, count)

    def forward_block(qi, count):
        queries = pair(q_all, qi)
        firsts = jnp.concatenate([first_ref[2 * qi], first_ref[2 * qi + 1]], axis=1)
        key_at = lax.broadcasted_iota(jnp.int32, (BLK, BLK), 0)
        query_at = lax.broadcasted_iota(jnp.int32, (BLK, BLK), 1)
        total = jnp.zeros((8, BLK), F32)
        for d in range(count):
            st = lax.dot_general(keys_of(0, qi - d), queries, last, preferred_element_type=F32)
            seen = key_at >= firsts - (qi - d) * BLK
            if d == 0:
                seen = seen & (key_at <= query_at)
            e = jnp.where(seen, jnp.exp2(st), 0.0)
            expo[d] = e
            total = total + fold(e)
        inv = 1.0 / jnp.sum(total, axis=0, keepdims=True)
        for d in range(count):
            prob[qi, d] = (expo[d] * inv).astype(BF16)

    def forward_step(i, carry):
        by_queries(i, forward_block)
        return carry

    lax.fori_loop(0, NBLK, forward_step, 0)

    def units(t, carry):
        cb, sb = cos_all[t], sin_all[t]
        q_unit[t] = turn_back(q_all[t].astype(F32), cb, sb)
        k_unit[t] = turn_back(kv_all[0, t].astype(F32), cb, sb)
        return carry

    lax.fori_loop(0, SEQ, units, 0)
    wait_on(g_all, recv_sem.at[0])

    def swap(kind, t):
        return pltpu.make_async_remote_copy(
            src_ref=dkv_buf.at[kind, t], dst_ref=mate.at[t],
            send_sem=swap_send, recv_sem=swap_recv.at[t],
            device_id=mate_at, device_id_type=MESH,
        )

    def value_block(kb, count):
        dv = jnp.dot(prob[kb, 0], pair(g_all, kb), preferred_element_type=F32)
        for d in range(1, count):
            dv = dv + jnp.dot(prob[kb + d, d], pair(g_all, kb + d), preferred_element_type=F32)
        dkv_buf[1, pl.ds(2 * kb, 2)] = dv.astype(BF16).reshape(2, TOK, HD)

    def value_step(i, carry):
        by_keys(i, value_block)
        kb = turns(i)

        @pl.when(core == 0)
        def _():
            swap(1, 2 * kb).start()
            swap(1, 2 * kb + 1).start()

        @pl.when(core == 1)
        def _():
            forward(2 * i, 0)
            forward(2 * i + 1, 0)

        return carry

    lax.fori_loop(0, NBLK, value_step, 0)

    @pl.when(core == 0)
    def _():
        wait_on(kv_all.at[1], pass_recv)

    slot_q = 2 * j_own + core
    slot_kv = core * 8 + j_own

    def homeward(kind, src, dst, t):
        return pltpu.make_async_remote_copy(
            src_ref=src, dst_ref=dst, send_sem=back_send.at[kind], recv_sem=back_recv.at[kind],
            device_id=(2 * z + span, t), device_id_type=MESH,
        )

    def back_part(kind, t):
        if kind == 0:
            return (0, dq_buf.at[t], dq_out.at[slot_q])
        return (1, mine.at[t], dkv_out.at[slot_kv])

    def home(t):
        return (span == core) & (t == s)

    def send_back(part, t):
        kind, src, dst = part

        @pl.when(home(t))
        def _():
            pltpu.make_async_copy(src, dst, back_recv.at[kind]).start()

        @pl.when(jnp.logical_not(home(t)))
        def _():
            homeward(kind, src, dst, t).start()

    def settle(kind, t):
        swap(kind, t).wait_recv()
        mine[t] = (dkv_buf[kind, t].astype(F32) + mate[t].astype(F32)).astype(BF16)
        send_back(back_part(1, t), t)

    def backward_block(qi, count):
        upstream = pair(g_all, qi)
        mixed = jnp.zeros((8, BLK), F32)
        for d in range(count):
            dpt = lax.dot_general(
                keys_of(1, qi - d), upstream, last, preferred_element_type=F32
            )
            pgrad[d] = dpt
            mixed = mixed + fold(prob[qi, d].astype(F32) * dpt)
        delta = jnp.sum(mixed, axis=0, keepdims=True)
        dq = jnp.zeros((BLK, HD), F32)
        for d in range(count):
            ds = (prob[qi, d].astype(F32) * (pgrad[d] - delta)).astype(BF16)
            prob[qi, d] = ds
            dq = dq + lax.dot_general(ds, keys_of(0, qi - d), lead, preferred_element_type=F32)
        dq_acc[...] = dq * SCALE

    def backward_step(i, carry):
        by_queries(i, backward_block)
        qi = turns(i)
        gain = gain_acc[...]
        for half in range(2):
            block = 2 * qi + half
            rows = dq_acc[half * TOK:(half + 1) * TOK, :]
            dq_buf[block] = rows.astype(BF16)
            send_back(back_part(0, block), block)
            both = turn_back(rows, cos_all[block], sin_all[block]) * q_unit[block]
            gain = gain + jnp.sum(both.reshape(TOK // 8, 8, HD), axis=0)
        gain_acc[...] = gain

        @pl.when(core == 1)
        def _():
            settle(1, 2 * qi)
            settle(1, 2 * qi + 1)

        return carry

    lax.fori_loop(0, NBLK, backward_step, 0)

    def key_block(kb, count):
        dk = jnp.dot(prob[kb, 0], pair(q_all, kb), preferred_element_type=F32)
        for d in range(1, count):
            dk = dk + jnp.dot(prob[kb + d, d], pair(q_all, kb + d), preferred_element_type=F32)
        dq_acc[...] = dk * LN2

    def key_step(i, gain):
        by_keys(i, key_block)
        kb = turns(i)
        dkv_buf[0, pl.ds(2 * kb, 2)] = dq_acc[...].astype(BF16).reshape(2, TOK, HD)

        @pl.when(core == 1)
        def _():
            swap(0, 2 * kb).start()
            swap(0, 2 * kb + 1).start()

        for half in range(2):
            block = 2 * kb + half
            rows = dq_acc[half * TOK:(half + 1) * TOK, :]
            both = turn_back(rows, cos_all[block], sin_all[block]) * k_unit[block]
            gain = gain + jnp.sum(both.reshape(TOK // 8, 8, HD), axis=0)

        @pl.when((core == 0) & (i > 0))
        def _():
            before = turns(i - 1)
            settle(0, 2 * before)
            settle(0, 2 * before + 1)

        return gain

    gain_k = lax.fori_loop(0, NBLK, key_step, jnp.zeros((8, HD), F32))
    row = lax.broadcasted_iota(jnp.int32, (8, HD), 0)
    gain_one[0] = jnp.where(
        row == 0,
        jnp.sum(gain_acc[...], axis=0, keepdims=True),
        jnp.where(row == 1, jnp.sum(gain_k, axis=0, keepdims=True), 0.0),
    )

    def share(stage, i):
        return pltpu.make_async_remote_copy(
            src_ref=gain_one.at[stage], dst_ref=stages.at[stage, rank[stage]],
            send_sem=stage_send, recv_sem=stage_recv.at[stage],
            device_id=member(stage, i), device_id_type=MESH,
        )

    def share_all(stage):
        def one(i, carry):
            @pl.when(i != rank[stage])
            def _():
                share(stage, i).start()

            return carry

        lax.fori_loop(0, 8, one, 0)
        stages[stage, rank[stage]] = gain_one[stage]

    def gathered(stage):
        wait_on(stages.at[stage, pl.ds(0, 7)], stage_recv.at[stage])
        return jnp.sum(stages[stage], axis=0)

    share_all(0)

    @pl.when(core == 0)
    def _():
        settle(0, 2 * turns(NBLK - 1))
        settle(0, 2 * turns(NBLK - 1) + 1)

    gain_one[1] = gathered(0)
    share_all(1)
    gain_one[2] = gathered(1)
    share_all(2)
    wait_on(kv_all.at[0], pass_send)
    wait_on(mate, swap_send)
    wait_on(stages.at[pl.ds(0, 3), pl.ds(0, 7)], stage_send)
    near_one = span == core

    @pl.when(near_one)
    def _():
        few = pl.ds(0, SEQ - 1)
        wait_on(g_buf.at[few], send_sem.at[0])
        wait_on(q_buf.at[few], send_sem.at[2])
        wait_on(seg_all.at[few], send_sem.at[3])
        wait_on(g_buf.at[few], send_sem.at[1])
        wait_on(dq_buf.at[few], back_send.at[0])
        wait_on(mine.at[few], back_send.at[1])

    @pl.when(jnp.logical_not(near_one))
    def _():
        wait_on(g_buf, send_sem.at[0])
        wait_on(q_buf, send_sem.at[2])
        wait_on(seg_all, send_sem.at[3])
        wait_on(g_buf, send_sem.at[1])
        wait_on(dq_buf, back_send.at[0])
        wait_on(mine, back_send.at[1])

    wait_on(dq_out, back_recv.at[0])
    wait_on(dkv_out, back_recv.at[1])
    total = gathered(2)
    gain_out[...] = jnp.where(
        row == 0, total / (qg_ref[...] * QMUL), total / kg_ref[...]
    )


def norm_kernel(
    where_ref, dq_ref, dkv_ref, q_ref, k_ref, qg_ref, kg_ref, gain_ref, near_ref, far_ref,
    gq_ref, gk_ref, gv_ref, gqg_ref, gkg_ref,
    q_wide, k_wide, q_new, k_new, v_new,
):
    cosine, sine = block_rope(near_ref, far_ref, where_ref[0])
    q_wide[...] = q_ref[...].astype(F32).reshape(TOK * 16, HD)
    k_wide[...] = k_ref[...].astype(F32).reshape(TOK * 8, HD)

    def back(wide, new, rows_at, upstream, gain):
        rows = wide[rows_at, :]
        size = lax.rsqrt(jnp.mean(rows * rows, axis=1, keepdims=True) + EPS)
        unit = rows * size
        slope = turn_back(upstream.astype(F32), cosine, sine) * gain
        new[rows_at, :] = size * (slope - unit * jnp.mean(slope * unit, axis=1, keepdims=True))

    for h in range(16):
        back(q_wide, q_new, pl.ds(h, TOK, stride=16), dq_ref[h], qg_ref[...])
    for j in range(8):
        back(k_wide, k_new, pl.ds(j, TOK, stride=8), dkv_ref[j], kg_ref[...])
        v_new[pl.ds(j, TOK, stride=8), :] = dkv_ref[8 + j].astype(F32)
    gq_ref[...] = q_new[...].reshape(TOK, 16, HD).astype(BF16)
    gk_ref[...] = k_new[...].reshape(TOK, 8, HD).astype(BF16)
    gv_ref[...] = v_new[...].reshape(TOK, 8, HD).astype(BF16)
    gqg_ref[...] = gain_ref[0:1, :]
    gkg_ref[...] = gain_ref[1:2, :]


def shape(dims, dtype):
    return jax.ShapeDtypeStruct(dims, dtype)


def body(q_pre, k_pre, values, grad_out, segment_ids, q_gain, k_gain):
    near, far = (jnp.asarray(table) for table in rope_tables())
    qg, kg = q_gain.reshape(1, HD), k_gain.reshape(1, HD)
    dma = pltpu.SemaphoreType.DMA
    tiles = (SEQ, TOK, HD)
    dq_back, dkv_back, gain_sums = pl.pallas_call(
        fused_kernel,
        name="heads_and_back",
        out_shape=(shape(tiles, BF16), shape(tiles, BF16), shape((8, HD), F32)),
        in_specs=[HBM] * 9,
        out_specs=(ANY, ANY, VM),
        scratch_shapes=[
            pltpu.VMEM((TOK, 16, HD), BF16), pltpu.VMEM((TOK, 8, HD), BF16),
            pltpu.VMEM((TOK, 8, HD), BF16), pltpu.VMEM((TOK, 16, HD), BF16),
            pltpu.VMEM((1, TOK), jnp.int32), pltpu.VMEM((1, HD), F32), pltpu.VMEM((1, HD), F32),
            pltpu.VMEM((2, TOK, HD), F32), pltpu.VMEM((SEQ, 2, HD), F32),
            pltpu.VMEM((TOK * 16, HD), F32), pltpu.VMEM((TOK * 8, HD), F32),
            pltpu.VMEM((TOK * 8, HD), F32), pltpu.VMEM((TOK * 16, HD), F32),
            pltpu.VMEM(tiles, BF16), pltpu.VMEM(tiles, BF16),
            pltpu.VMEM((2, 8, TOK, HD), BF16),
            pltpu.VMEM(tiles, BF16), pltpu.VMEM(tiles, BF16), pltpu.VMEM((2,) + tiles, BF16),
            pltpu.VMEM((SEQ, 1, TOK), jnp.int32), pltpu.VMEM((SEQ, 1, TOK), jnp.int32),
            pltpu.VMEM(tiles, F32), pltpu.VMEM(tiles, F32),
            pltpu.VMEM(tiles, F32), pltpu.VMEM(tiles, F32),
            pltpu.VMEM((BAND, BLK, BLK), F32), pltpu.VMEM((NBLK, BAND, BLK, BLK), BF16),
            pltpu.VMEM((BAND, BLK, BLK), F32), pltpu.VMEM((BLK, HD), F32),
            pltpu.VMEM((8, HD), F32),
            pltpu.VMEM(tiles, BF16), pltpu.VMEM((2,) + tiles, BF16),
            pltpu.VMEM(tiles, BF16), pltpu.VMEM(tiles, BF16),
            pltpu.VMEM((3, 8, HD), F32), pltpu.VMEM((3, 8, 8, HD), F32),
            dma((9,)), dma((4,)), dma((4,)), dma, dma, dma((SEQ,)),
            dma((2,)), dma((2,)), dma, dma((SEQ,)), dma, dma((3,)),
        ],
        compiler_params=pltpu.CompilerParams(
            collective_id=0, has_side_effects=True, vmem_limit_bytes=48 << 20
        ),
    )(*(
        pltpu.with_memory_space_constraint(x, pltpu.HBM)
        for x in (
            q_pre[0], k_pre[0], values[0], grad_out[0], segment_ids, qg, kg, near, far
        )
    ))

    where = lax.axis_index("seq").astype(jnp.int32).reshape(1)
    grad_q, grad_k, grad_v, grad_qg, grad_kg = pl.pallas_call(
        norm_kernel,
        name="norm_back",
        out_shape=(
            shape((TOK, 16, HD), BF16), shape((TOK, 8, HD), BF16), shape((TOK, 8, HD), BF16),
            shape((1, HD), F32), shape((1, HD), F32),
        ),
        in_specs=[pl.BlockSpec(memory_space=pltpu.SMEM)] + [VM] * 9,
        out_specs=(VM,) * 5,
        scratch_shapes=[
            pltpu.VMEM((TOK * 16, HD), F32), pltpu.VMEM((TOK * 8, HD), F32),
            pltpu.VMEM((TOK * 16, HD), F32), pltpu.VMEM((TOK * 8, HD), F32),
            pltpu.VMEM((TOK * 8, HD), F32),
        ],
        compiler_params=pltpu.CompilerParams(vmem_limit_bytes=32 << 20),
    )(where, dq_back, dkv_back, q_pre[0], k_pre[0], qg, kg, gain_sums, near, far)
    return (
        grad_q[None], grad_k[None], grad_v[None], grad_qg.reshape(HD), grad_kg.reshape(HD)
    )


def solution(mesh):
    tokens = P("dp", "seq", None, None)
    return jax.shard_map(
        body,
        mesh=mesh,
        in_specs=(tokens, tokens, tokens, tokens, P("dp", "seq"), P(), P()),
        out_specs=(tokens, tokens, tokens, P(), P()),
        check_vma=False,
    )
```

```python
import jax
import jax.numpy as jnp
import numpy as np
from jax import lax
from jax.experimental import pallas as pl
from jax.experimental.pallas import tpu as pltpu
from jax.sharding import PartitionSpec as P

PRESCALE = 168
HD = 128
SEQ = 16
TOK = 128
TOTAL = SEQ * TOK
BLK = 256
NBLK = TOTAL // BLK
BAND = 5
EPS = 1e-6
ROPE_BASE = 1000000.0
ROPE_FACTOR = 8.0
SCALE = float(PRESCALE) ** (-0.5)
QMUL = SCALE * float(np.log2(np.e))
LN2 = float(np.log(2.0))
MESH = pl.DeviceIdType.MESH
F32 = jnp.float32
BF16 = jnp.bfloat16
ANY = pl.BlockSpec(memory_space=pl.ANY)
HBM = pl.BlockSpec(memory_space=pltpu.HBM)


def rope_tables():
    half = HD // 2
    freqs = ROPE_BASE ** (-(np.arange(half, dtype=np.float64) * 2.0 / HD))
    freqs = np.concatenate([freqs, freqs])
    near = np.arange(TOK, dtype=np.float64)[:, None] / ROPE_FACTOR * freqs[None, :]
    far = np.arange(SEQ, dtype=np.float64)[:, None] * TOK / ROPE_FACTOR * freqs[None, :]
    return (
        np.stack([np.cos(near), np.sin(near)]).astype(np.float32),
        np.stack([np.cos(far), np.sin(far)], axis=1).astype(np.float32),
    )


def block_rope(near_ref, far_ref, block):
    far = far_ref[block]
    cb, sb = far[0:1, :], far[1:2, :]
    cosine = near_ref[0] * cb - near_ref[1] * sb
    sine = near_ref[1] * cb + near_ref[0] * sb
    lane = lax.broadcasted_iota(jnp.int32, (TOK, HD), 1)
    return cosine, jnp.where(lane < HD // 2, -sine, sine)


def turn(rows, cosine, sine):
    return rows * cosine + pltpu.roll(rows, HD // 2, 1) * sine


def turn_back(rows, cosine, sine):
    return rows * cosine - pltpu.roll(rows, HD // 2, 1) * sine


def place():
    dp = lax.axis_index("dp")
    s = lax.axis_index("seq")
    z = lax.div(dp, 2)
    return dp, s, z, lax.rem(dp, 2)


def fused_kernel(
    q_hbm, k_hbm, v_hbm, g_hbm, seg_hbm, qg_hbm, kg_hbm, near_hbm, far_hbm,
    gq_out, gk_out, gv_out, gqg_out, gkg_out,
    q_raw, k_raw, v_raw, g_raw, seg_one, qg_ref, kg_ref, near_ref, far_ref,
    q_wide, k_wide, v_wide, g_wide, q_row, k_row, q_size, k_size, q_buf, g_buf, kv_buf,
    q_all, g_all, kv_all, seg_all, first_ref, cos_all, sin_all, q_unit, k_unit,
    expo, prob, sgrad, pgrad, dq_acc, gain_acc,
    dq_buf, dkv_buf, mate, mine, dq_out, dkv_out, gain_one, stages,
    load_sem, send_sem, recv_sem, pass_send, pass_recv, pass_got,
    back_send, back_recv, swap_send, swap_recv, stage_send, stage_recv,
):
    dp, s, z, core = place()
    j_own = lax.div(s, 2)
    span = lax.rem(s, 2)
    mate_at = (2 * z + 1 - core, s)
    loads = [
        pltpu.make_async_copy(src, dst, load_sem.at[i])
        for i, (src, dst) in enumerate(
            (
                (k_hbm, k_raw), (near_hbm, near_ref), (far_hbm, far_ref), (kg_hbm, kg_ref),
                (qg_hbm, qg_ref), (seg_hbm, seg_one), (q_hbm, q_raw), (v_hbm, v_raw),
                (g_hbm, g_raw),
            )
        )
    ]
    for copy in loads:
        copy.start()
    barrier = pltpu.get_barrier_semaphore()

    def greet(i, carry):
        @pl.when(i != core * SEQ + s)
        def _():
            pl.semaphore_signal(
                barrier, inc=1, device_id=(2 * z + lax.div(i, SEQ), lax.rem(i, SEQ)),
                device_id_type=MESH,
            )

        return carry

    sizes = (16, 32)
    rank = (z, core * SEQ + s)

    def member(stage, i):
        if stage == 0:
            return (2 * i + core, s)
        return (2 * z + lax.div(i, SEQ), lax.rem(i, SEQ))

    def greet_z(i, carry):
        @pl.when(i != z)
        def _():
            pl.semaphore_signal(barrier, inc=1, device_id=member(0, i), device_id_type=MESH)

        return carry

    lax.fori_loop(0, 2 * SEQ, greet, 0)
    lax.fori_loop(0, 16, greet_z, 0)
    for copy in loads[:6]:
        copy.wait()
    cosine, sine = block_rope(near_ref, far_ref, s)
    k_wide[...] = k_raw[...].astype(F32).reshape(TOK * 8, HD)

    def prepare(wide, rows_at, gain, row, size_at):
        rows = wide[rows_at, :]
        size = lax.rsqrt(jnp.mean(rows * rows, axis=1, keepdims=True) + EPS)
        unit = rows * size
        row[...] = unit
        size_at[...] = jnp.broadcast_to(size, (TOK, HD))
        return turn(unit * gain, cosine, sine)

    for j in range(8):
        kv_buf[0, j] = prepare(
            k_wide, pl.ds(j, TOK, stride=8), kg_ref[...], k_row.at[j], k_size.at[j]
        ).astype(BF16)
    pl.semaphore_wait(barrier, 2 * SEQ - 1 + 15)

    def is_me(j, r):
        return (2 * z + r == dp) & (2 * j + core == s)

    def landing(kind):
        return recv_sem.at[kind] if kind != 1 else pass_got.at[s]

    def outward(kind, src, dst, j, r):
        return pltpu.make_async_remote_copy(
            src_ref=src, dst_ref=dst, send_sem=send_sem.at[kind], recv_sem=landing(kind),
            device_id=(2 * z + r, 2 * j + core), device_id_type=MESH,
        )

    def send(part, j, r):
        kind, src, dst = part
        me = is_me(j, r)

        @pl.when(me)
        def _():
            pltpu.make_async_copy(src, dst, landing(kind)).start()

        @pl.when(jnp.logical_not(me))
        def _():
            outward(kind, src, dst, j, r).start()

    def part_of(kind, j, r):
        h = 2 * j + r
        if kind == 0:
            return (0, g_buf.at[h], g_all.at[s])
        if kind == 1:
            return (1, kv_buf.at[r, j], kv_all.at[r, s])
        if kind == 2:
            return (2, q_buf.at[h], q_all.at[s])
        return (3, seg_one, seg_all.at[s])

    def turns(t):
        return lax.rem(j_own + t, SEQ // 2)

    def send_k(t, carry):
        j = turns(t)
        send(part_of(1, j, 0), j, 0)
        return carry

    lax.fori_loop(0, 8, send_k, 0)
    loads[6].wait()
    q_wide[...] = q_raw[...].astype(F32).reshape(TOK * 16, HD)

    def send_q(t, carry):
        j = turns(t)
        for r in range(2):
            h = 2 * j + r
            q_buf[h] = (prepare(
                q_wide, pl.ds(h, TOK, stride=16), qg_ref[...], q_row.at[h], q_size.at[h]
            ) * QMUL).astype(BF16)
            send(part_of(2, j, r), j, r)
        return carry

    lax.fori_loop(0, 8, send_q, 0)

    def send_seg(t, carry):
        j = turns(t)
        for r in range(2):
            send(part_of(3, j, r), j, r)
        return carry

    lax.fori_loop(0, 8, send_seg, 0)
    loads[7].wait()
    v_wide[...] = v_raw[...].astype(F32).reshape(TOK * 8, HD)

    def send_v(t, carry):
        j = turns(t)
        kv_buf[1, j] = v_wide[pl.ds(j, TOK, stride=8), :].astype(BF16)
        send(part_of(1, j, 1), j, 1)
        return carry

    lax.fori_loop(0, 8, send_v, 0)
    loads[8].wait()
    g_wide[...] = g_raw[...].astype(F32).reshape(TOK * 16, HD)

    def send_g(t, carry):
        j = turns(t)
        for r in range(2):
            h = 2 * j + r
            g_buf[h] = g_wide[pl.ds(h, TOK, stride=16), :].astype(BF16)
            send(part_of(0, j, r), j, r)
        return carry

    lax.fori_loop(0, 8, send_g, 0)

    def passing(kind, t):
        return pltpu.make_async_remote_copy(
            src_ref=kv_all.at[kind, t], dst_ref=kv_all.at[kind, t],
            send_sem=pass_send, recv_sem=pass_recv,
            device_id=mate_at, device_id_type=MESH,
        )

    def wait_on(ref, sem):
        pltpu.make_async_copy(ref, ref, sem).wait()

    def forward(i, carry):
        t = lax.rem(2 * (j_own + SEQ // 2 - lax.div(i, 2)) + lax.rem(i, 2), SEQ)
        wait_on(kv_all.at[core, t], pass_got.at[t])
        passing(core, t).start()
        return carry

    def tables(t, carry):
        cb, sb = block_rope(near_ref, far_ref, t)
        cos_all[t] = cb
        sin_all[t] = sb
        return carry

    lax.fori_loop(0, SEQ, tables, 0)

    @pl.when(core == 0)
    def _():
        lax.fori_loop(0, SEQ, forward, 0)

    wait_on(q_all, recv_sem.at[2])
    wait_on(seg_all, recv_sem.at[3])

    @pl.when(core == 1)
    def _():
        wait_on(kv_all.at[0], pass_recv)

    seg = seg_all[...].reshape(SEQ, TOK)
    first = jnp.zeros((SEQ, TOK), F32)
    for d in range(1, 8):
        below = jnp.where(seg < d, 1.0, 0.0)
        count = jnp.sum(jnp.sum(below, axis=1, keepdims=True), axis=0, keepdims=True)
        first = jnp.where(seg == d, count, first)
    first_ref[...] = first.astype(jnp.int32).reshape(SEQ, 1, TOK)
    gain_acc[...] = jnp.zeros_like(gain_acc)
    last = (((1,), (1,)), ((), ()))
    lead = (((0,), (0,)), ((), ()))

    def pair(ref, qi):
        return ref[pl.ds(2 * qi, 2)].reshape(BLK, HD)

    def keys_of(kind, kb):
        return kv_all[kind, pl.ds(2 * kb, 2)].reshape(BLK, HD)

    def fold(x):
        return jnp.sum(x.reshape(BLK // 8, 8, BLK), axis=0)

    def by_queries(i, run):
        qi = turns(i)
        for count in range(1, BAND + 1):
            fits = (qi >= BAND - 1) if count == BAND else (qi == count - 1)

            @pl.when(fits)
            def _(count=count):
                run(qi, count)

    def by_keys(i, run):
        kb = turns(i)
        for count in range(1, BAND + 1):
            fits = (kb <= NBLK - BAND) if count == BAND else (kb == NBLK - count)

            @pl.when(fits)
            def _(count=count):
                run(kb, count)

    def forward_block(qi, count):
        queries = pair(q_all, qi)
        firsts = jnp.concatenate([first_ref[2 * qi], first_ref[2 * qi + 1]], axis=1)
        key_at = lax.broadcasted_iota(jnp.int32, (BLK, BLK), 0)
        query_at = lax.broadcasted_iota(jnp.int32, (BLK, BLK), 1)
        total = jnp.zeros((8, BLK), F32)
        for d in range(count):
            st = lax.dot_general(keys_of(0, qi - d), queries, last, preferred_element_type=F32)
            seen = key_at >= firsts - (qi - d) * BLK
            if d == 0:
                seen = seen & (key_at <= query_at)
            e = jnp.where(seen, jnp.exp2(st), 0.0)
            expo[d] = e
            total = total + fold(e)
        inv = 1.0 / jnp.sum(total, axis=0, keepdims=True)
        for d in range(count):
            prob[qi, d] = (expo[d] * inv).astype(BF16)

    def forward_step(i, carry):
        by_queries(i, forward_block)

        @pl.when(core == 1)
        def _():
            forward(2 * i, 0)
            forward(2 * i + 1, 0)

        return carry

    lax.fori_loop(0, NBLK, forward_step, 0)

    def units(t, carry):
        cb, sb = cos_all[t], sin_all[t]
        q_unit[t] = turn_back(q_all[t].astype(F32), cb, sb)
        k_unit[t] = turn_back(kv_all[0, t].astype(F32), cb, sb)
        return carry

    lax.fori_loop(0, SEQ, units, 0)
    wait_on(g_all, recv_sem.at[0])

    @pl.when(core == 0)
    def _():
        wait_on(kv_all.at[1], pass_recv)

    def swap(kind, t):
        return pltpu.make_async_remote_copy(
            src_ref=dkv_buf.at[kind, t], dst_ref=mate.at[t],
            send_sem=swap_send, recv_sem=swap_recv.at[t],
            device_id=mate_at, device_id_type=MESH,
        )

    slot_q = 2 * j_own + core
    slot_kv = core * 8 + j_own

    def homeward(kind, src, dst, t):
        return pltpu.make_async_remote_copy(
            src_ref=src, dst_ref=dst, send_sem=back_send.at[kind], recv_sem=back_recv.at[kind],
            device_id=(2 * z + span, t), device_id_type=MESH,
        )

    def back_part(kind, t):
        if kind == 0:
            return (0, dq_buf.at[t], dq_out.at[slot_q])
        return (1, mine.at[t], dkv_out.at[slot_kv])

    def home(t):
        return (span == core) & (t == s)

    def send_back(part, t):
        kind, src, dst = part

        @pl.when(home(t))
        def _():
            pltpu.make_async_copy(src, dst, back_recv.at[kind]).start()

        @pl.when(jnp.logical_not(home(t)))
        def _():
            homeward(kind, src, dst, t).start()

    def settle(kind, t):
        swap(kind, t).wait_recv()
        mine[t] = (dkv_buf[kind, t].astype(F32) + mate[t].astype(F32)).astype(BF16)
        send_back(back_part(1, t), t)

    def settle_pair(kind, i):
        settle(kind, 2 * turns(i))
        settle(kind, 2 * turns(i) + 1)

    def backward_block(qi, count):
        upstream = pair(g_all, qi)
        mixed = jnp.zeros((8, BLK), F32)
        for d in range(count):
            dpt = lax.dot_general(
                keys_of(1, qi - d), upstream, last, preferred_element_type=F32
            )
            pgrad[d] = dpt
            mixed = mixed + fold(prob[qi, d].astype(F32) * dpt)
        delta = jnp.sum(mixed, axis=0, keepdims=True)
        dq = jnp.zeros((BLK, HD), F32)
        for d in range(count):
            ds = (prob[qi, d].astype(F32) * (pgrad[d] - delta)).astype(BF16)
            sgrad[qi, d] = ds
            dq = dq + lax.dot_general(ds, keys_of(0, qi - d), lead, preferred_element_type=F32)
        dq_acc[...] = dq * SCALE

    def backward_step(i, carry):
        by_queries(i, backward_block)
        qi = turns(i)
        gain = gain_acc[...]
        for half in range(2):
            block = 2 * qi + half
            rows = dq_acc[half * TOK:(half + 1) * TOK, :]
            dq_buf[block] = rows.astype(BF16)
            send_back(back_part(0, block), block)
            both = turn_back(rows, cos_all[block], sin_all[block]) * q_unit[block]
            gain = gain + jnp.sum(both.reshape(TOK // 8, 8, HD), axis=0)
        gain_acc[...] = gain

        return carry

    lax.fori_loop(0, NBLK, backward_step, 0)

    def key_block(kb, count):
        dk = jnp.dot(sgrad[kb, 0], pair(q_all, kb), preferred_element_type=F32)
        for d in range(1, count):
            dk = dk + jnp.dot(sgrad[kb + d, d], pair(q_all, kb + d), preferred_element_type=F32)
        dq_acc[...] = dk * LN2

    def key_step(i, gain):
        by_keys(i, key_block)
        kb = turns(i)
        dkv_buf[0, pl.ds(2 * kb, 2)] = dq_acc[...].astype(BF16).reshape(2, TOK, HD)

        @pl.when(core == 1)
        def _():
            swap(0, 2 * kb).start()
            swap(0, 2 * kb + 1).start()

        for half in range(2):
            block = 2 * kb + half
            rows = dq_acc[half * TOK:(half + 1) * TOK, :]
            both = turn_back(rows, cos_all[block], sin_all[block]) * k_unit[block]
            gain = gain + jnp.sum(both.reshape(TOK // 8, 8, HD), axis=0)

        @pl.when((core == 0) & (i > 0))
        def _():
            settle_pair(0, i - 1)

        return gain

    gain_k = lax.fori_loop(0, NBLK, key_step, jnp.zeros((8, HD), F32))
    row = lax.broadcasted_iota(jnp.int32, (8, HD), 0)
    gain_one[0] = jnp.where(
        row == 0,
        jnp.sum(gain_acc[...], axis=0, keepdims=True),
        jnp.where(row == 1, jnp.sum(gain_k, axis=0, keepdims=True), 0.0),
    )

    def share(stage, i):
        return pltpu.make_async_remote_copy(
            src_ref=gain_one.at[stage], dst_ref=stages.at[stage, rank[stage]],
            send_sem=stage_send.at[stage], recv_sem=stage_recv.at[stage],
            device_id=member(stage, i), device_id_type=MESH,
        )

    def share_all(stage):
        def one(i, carry):
            @pl.when(i != rank[stage])
            def _():
                share(stage, i).start()

            return carry

        lax.fori_loop(0, sizes[stage], one, 0)
        stages[stage, rank[stage]] = gain_one[stage]

    def gathered(stage):
        wait_on(stages.at[stage, pl.ds(0, sizes[stage] - 1)], stage_recv.at[stage])
        return jnp.sum(stages[stage, 0:sizes[stage]], axis=0)

    share_all(0)

    @pl.when(core == 0)
    def _():
        settle_pair(0, NBLK - 1)

    def value_block(kb, count):
        dv = jnp.dot(prob[kb, 0], pair(g_all, kb), preferred_element_type=F32)
        for d in range(1, count):
            dv = dv + jnp.dot(prob[kb + d, d], pair(g_all, kb + d), preferred_element_type=F32)
        dkv_buf[1, pl.ds(2 * kb, 2)] = dv.astype(BF16).reshape(2, TOK, HD)

    def value_step(i, carry):
        by_keys(i, value_block)
        kb = turns(i)

        @pl.when(core == 0)
        def _():
            swap(1, 2 * kb).start()
            swap(1, 2 * kb + 1).start()

        @pl.when((core == 1) & (i > 0))
        def _():
            settle_pair(1, i - 1)

        return carry

    lax.fori_loop(0, NBLK, value_step, 0)

    @pl.when(core == 1)
    def _():
        settle_pair(1, NBLK - 1)

    gain_one[1] = gathered(0)
    share_all(1)

    def norm_back(upstream, gain, unit, size):
        slope = turn_back(upstream.astype(F32), cosine, sine) * gain
        return size * (slope - unit * jnp.mean(slope * unit, axis=1, keepdims=True))

    wait_on(dq_out, back_recv.at[0])
    for h in range(16):
        q_wide[pl.ds(h, TOK, stride=16), :] = norm_back(
            dq_out[h], qg_ref[...], q_row[h], q_size[h]
        )
    gq_out[...] = q_wide[...].reshape(TOK, 16, HD).astype(BF16)
    wait_on(dkv_out, back_recv.at[1])
    for j in range(8):
        k_wide[pl.ds(j, TOK, stride=8), :] = norm_back(
            dkv_out[j], kg_ref[...], k_row[j], k_size[j]
        )
    gk_out[...] = k_wide[...].reshape(TOK, 8, HD).astype(BF16)
    for j in range(8):
        v_wide[pl.ds(j, TOK, stride=8), :] = dkv_out[8 + j].astype(F32)
    gv_out[...] = v_wide[...].reshape(TOK, 8, HD).astype(BF16)
    wait_on(kv_all.at[0], pass_send)
    wait_on(mate, swap_send)
    wait_on(stages.at[0, pl.ds(0, 15)], stage_send.at[0])
    near_one = span == core

    @pl.when(near_one)
    def _():
        few = pl.ds(0, SEQ - 1)
        wait_on(g_buf.at[few], send_sem.at[0])
        wait_on(q_buf.at[few], send_sem.at[2])
        wait_on(seg_all.at[few], send_sem.at[3])
        wait_on(g_buf.at[few], send_sem.at[1])
        wait_on(dq_buf.at[few], back_send.at[0])
        wait_on(mine.at[few], back_send.at[1])

    @pl.when(jnp.logical_not(near_one))
    def _():
        wait_on(g_buf, send_sem.at[0])
        wait_on(q_buf, send_sem.at[2])
        wait_on(seg_all, send_sem.at[3])
        wait_on(g_buf, send_sem.at[1])
        wait_on(dq_buf, back_send.at[0])
        wait_on(mine, back_send.at[1])

    wait_on(stages.at[1, pl.ds(0, 31)], stage_send.at[1])
    total = gathered(1)
    gqg_out[...] = total[0:1, :] / (qg_ref[...] * QMUL)
    gkg_out[...] = total[1:2, :] / kg_ref[...]


def shape(dims, dtype):
    return jax.ShapeDtypeStruct(dims, dtype)


def body(q_pre, k_pre, values, grad_out, segment_ids, q_gain, k_gain):
    near, far = (jnp.asarray(table) for table in rope_tables())
    qg, kg = q_gain.reshape(1, HD), k_gain.reshape(1, HD)
    dma = pltpu.SemaphoreType.DMA
    tiles = (SEQ, TOK, HD)
    kinds = (
        shape((TOK, 16, HD), BF16), shape((TOK, 8, HD), BF16), shape((TOK, 8, HD), BF16),
        shape((1, HD), F32), shape((1, HD), F32),
    )
    grad_q, grad_k, grad_v, grad_qg, grad_kg = pl.pallas_call(
        fused_kernel,
        name="heads_and_back",
        out_shape=kinds,
        in_specs=[HBM] * 9,
        out_specs=(pl.BlockSpec(memory_space=pltpu.VMEM),) * 5,
        scratch_shapes=[
            pltpu.VMEM((TOK, 16, HD), BF16), pltpu.VMEM((TOK, 8, HD), BF16),
            pltpu.VMEM((TOK, 8, HD), BF16), pltpu.VMEM((TOK, 16, HD), BF16),
            pltpu.VMEM((1, TOK), jnp.int32), pltpu.VMEM((1, HD), F32), pltpu.VMEM((1, HD), F32),
            pltpu.VMEM((2, TOK, HD), F32), pltpu.VMEM((SEQ, 2, HD), F32),
            pltpu.VMEM((TOK * 16, HD), F32), pltpu.VMEM((TOK * 8, HD), F32),
            pltpu.VMEM((TOK * 8, HD), F32), pltpu.VMEM((TOK * 16, HD), F32),
            pltpu.VMEM(tiles, F32), pltpu.VMEM((8, TOK, HD), F32),
            pltpu.VMEM(tiles, F32), pltpu.VMEM((8, TOK, HD), F32),
            pltpu.VMEM(tiles, BF16), pltpu.VMEM(tiles, BF16),
            pltpu.VMEM((2, 8, TOK, HD), BF16),
            pltpu.VMEM(tiles, BF16), pltpu.VMEM(tiles, BF16), pltpu.VMEM((2,) + tiles, BF16),
            pltpu.VMEM((SEQ, 1, TOK), jnp.int32), pltpu.VMEM((SEQ, 1, TOK), jnp.int32),
            pltpu.VMEM(tiles, F32), pltpu.VMEM(tiles, F32),
            pltpu.VMEM(tiles, F32), pltpu.VMEM(tiles, F32),
            pltpu.VMEM((BAND, BLK, BLK), F32), pltpu.VMEM((NBLK, BAND, BLK, BLK), BF16),
            pltpu.VMEM((NBLK, BAND, BLK, BLK), BF16),
            pltpu.VMEM((BAND, BLK, BLK), F32), pltpu.VMEM((BLK, HD), F32),
            pltpu.VMEM((8, HD), F32),
            pltpu.VMEM(tiles, BF16), pltpu.VMEM((2,) + tiles, BF16),
            pltpu.VMEM(tiles, BF16), pltpu.VMEM(tiles, BF16),
            pltpu.VMEM(tiles, BF16), pltpu.VMEM(tiles, BF16),
            pltpu.VMEM((2, 8, HD), F32), pltpu.VMEM((2, 32, 8, HD), F32),
            dma((9,)), dma((4,)), dma((4,)), dma, dma, dma((SEQ,)),
            dma((2,)), dma((2,)), dma, dma((SEQ,)), dma((2,)), dma((2,)),
        ],
        compiler_params=pltpu.CompilerParams(
            collective_id=0, has_side_effects=True, vmem_limit_bytes=48 << 20
        ),
    )(*(
        pltpu.with_memory_space_constraint(x, pltpu.HBM)
        for x in (
            q_pre[0], k_pre[0], values[0], grad_out[0], segment_ids, qg, kg, near, far
        )
    ))

    return (
        grad_q[None], grad_k[None], grad_v[None], grad_qg.reshape(HD), grad_kg.reshape(HD)
    )


def solution(mesh):
    tokens = P("dp", "seq", None, None)
    return jax.shard_map(
        body,
        mesh=mesh,
        in_specs=(tokens, tokens, tokens, tokens, P("dp", "seq"), P(), P()),
        out_specs=(tokens, tokens, tokens, P(), P()),
        check_vma=False,
    )
```

```python
import jax
import jax.numpy as jnp
import numpy as np
from jax import lax
from jax.experimental import pallas as pl
from jax.experimental.pallas import tpu as pltpu
from jax.sharding import PartitionSpec as P

PRESCALE = 168
HD = 128
SEQ = 16
TOK = 128
TOTAL = SEQ * TOK
BLK = 256
NBLK = TOTAL // BLK
BAND = 5
EPS = 1e-6
ROPE_BASE = 1000000.0
ROPE_FACTOR = 8.0
SCALE = float(PRESCALE) ** (-0.5)
QMUL = SCALE * float(np.log2(np.e))
LN2 = float(np.log(2.0))
MESH = pl.DeviceIdType.MESH
F32 = jnp.float32
BF16 = jnp.bfloat16
ANY = pl.BlockSpec(memory_space=pl.ANY)
HBM = pl.BlockSpec(memory_space=pltpu.HBM)


def rope_tables():
    half = HD // 2
    freqs = ROPE_BASE ** (-(np.arange(half, dtype=np.float64) * 2.0 / HD))
    freqs = np.concatenate([freqs, freqs])
    near = np.arange(TOK, dtype=np.float64)[:, None] / ROPE_FACTOR * freqs[None, :]
    far = np.arange(SEQ, dtype=np.float64)[:, None] * TOK / ROPE_FACTOR * freqs[None, :]
    return (
        np.stack([np.cos(near), np.sin(near)]).astype(np.float32),
        np.stack([np.cos(far), np.sin(far)], axis=1).astype(np.float32),
    )


def block_rope(near_ref, far_ref, block):
    far = far_ref[block]
    cb, sb = far[0:1, :], far[1:2, :]
    cosine = near_ref[0] * cb - near_ref[1] * sb
    sine = near_ref[1] * cb + near_ref[0] * sb
    lane = lax.broadcasted_iota(jnp.int32, (TOK, HD), 1)
    return cosine, jnp.where(lane < HD // 2, -sine, sine)


def turn(rows, cosine, sine):
    return rows * cosine + pltpu.roll(rows, HD // 2, 1) * sine


def turn_back(rows, cosine, sine):
    return rows * cosine - pltpu.roll(rows, HD // 2, 1) * sine


def place():
    dp = lax.axis_index("dp")
    s = lax.axis_index("seq")
    z = lax.div(dp, 2)
    return dp, s, z, lax.rem(dp, 2)


def fused_kernel(
    q_hbm, k_hbm, v_hbm, g_hbm, seg_hbm, qg_hbm, kg_hbm, near_hbm, far_hbm,
    gq_out, gk_out, gv_out, gqg_out, gkg_out,
    q_raw, k_raw, v_raw, g_raw, seg_one, qg_ref, kg_ref, near_ref, far_ref,
    q_wide, k_wide, v_wide, g_wide, q_row, k_row, q_size, k_size, q_buf, g_buf, kv_buf,
    q_all, g_all, kv_all, seg_all, first_ref, cos_all, sin_all, q_unit, k_unit,
    expo, prob, sgrad, pgrad, dq_acc, gain_acc,
    dq_buf, dkv_buf, mate, mine, dq_out, dkv_out, gain_one, stages, gain_two,
    load_sem, send_sem, recv_sem, pass_send, pass_recv, pass_got, g_got,
    back_send, back_recv, swap_send, swap_recv, stage_send, stage_recv, store_sem,
):
    dp, s, z, core = place()
    j_own = lax.div(s, 2)
    span = lax.rem(s, 2)
    mate_at = (2 * z + 1 - core, s)
    loads = [
        pltpu.make_async_copy(src, dst, load_sem.at[i])
        for i, (src, dst) in enumerate(
            (
                (k_hbm, k_raw), (near_hbm, near_ref), (far_hbm, far_ref), (kg_hbm, kg_ref),
                (qg_hbm, qg_ref), (seg_hbm, seg_one), (q_hbm, q_raw), (v_hbm, v_raw),
                (g_hbm, g_raw),
            )
        )
    ]
    for copy in loads:
        copy.start()
    barrier = pltpu.get_barrier_semaphore()

    def greet(i, carry):
        @pl.when(i != core * SEQ + s)
        def _():
            pl.semaphore_signal(
                barrier, inc=1, device_id=(2 * z + lax.div(i, SEQ), lax.rem(i, SEQ)),
                device_id_type=MESH,
            )

        return carry

    sizes = (16, 32)
    rank = (z, core * SEQ + s)

    def member(stage, i):
        if stage == 0:
            return (2 * i + core, s)
        return (2 * z + lax.div(i, SEQ), lax.rem(i, SEQ))

    def greet_z(i, carry):
        @pl.when(i != z)
        def _():
            pl.semaphore_signal(barrier, inc=1, device_id=member(0, i), device_id_type=MESH)

        return carry

    lax.fori_loop(0, 2 * SEQ, greet, 0)
    lax.fori_loop(0, 16, greet_z, 0)
    for copy in loads[:6]:
        copy.wait()
    cosine, sine = block_rope(near_ref, far_ref, s)
    k_wide[...] = k_raw[...].astype(F32).reshape(TOK * 8, HD)

    def prepare(wide, rows_at, gain, row, size_at):
        rows = wide[rows_at, :]
        size = lax.rsqrt(jnp.mean(rows * rows, axis=1, keepdims=True) + EPS)
        unit = rows * size
        row[...] = unit
        size_at[...] = jnp.broadcast_to(size, (TOK, HD))
        return turn(unit * gain, cosine, sine)

    for j in range(8):
        kv_buf[0, j] = prepare(
            k_wide, pl.ds(j, TOK, stride=8), kg_ref[...], k_row.at[j], k_size.at[j]
        ).astype(BF16)
    pl.semaphore_wait(barrier, 2 * SEQ - 1 + 15)

    def is_me(j, r):
        return (2 * z + r == dp) & (2 * j + core == s)

    def landing(kind):
        if kind == 0:
            return g_got.at[s]
        return recv_sem.at[kind] if kind != 1 else pass_got.at[s]

    def outward(kind, src, dst, j, r):
        return pltpu.make_async_remote_copy(
            src_ref=src, dst_ref=dst, send_sem=send_sem.at[kind], recv_sem=landing(kind),
            device_id=(2 * z + r, 2 * j + core), device_id_type=MESH,
        )

    def send(part, j, r):
        kind, src, dst = part
        me = is_me(j, r)

        @pl.when(me)
        def _():
            pltpu.make_async_copy(src, dst, landing(kind)).start()

        @pl.when(jnp.logical_not(me))
        def _():
            outward(kind, src, dst, j, r).start()

    def part_of(kind, j, r):
        h = 2 * j + r
        if kind == 0:
            return (0, g_buf.at[h], g_all.at[s])
        if kind == 1:
            return (1, kv_buf.at[r, j], kv_all.at[r, s])
        if kind == 2:
            return (2, q_buf.at[h], q_all.at[s])
        return (3, seg_one, seg_all.at[s])

    def turns(t):
        return lax.rem(j_own + t, SEQ // 2)

    def send_k(t, carry):
        j = turns(t)
        send(part_of(1, j, 0), j, 0)
        return carry

    lax.fori_loop(0, 8, send_k, 0)
    loads[6].wait()
    q_wide[...] = q_raw[...].astype(F32).reshape(TOK * 16, HD)

    def send_q(t, carry):
        j = turns(t)
        for r in range(2):
            h = 2 * j + r
            q_buf[h] = (prepare(
                q_wide, pl.ds(h, TOK, stride=16), qg_ref[...], q_row.at[h], q_size.at[h]
            ) * QMUL).astype(BF16)
            send(part_of(2, j, r), j, r)
        return carry

    lax.fori_loop(0, 8, send_q, 0)

    def send_seg(t, carry):
        j = turns(t)
        for r in range(2):
            send(part_of(3, j, r), j, r)
        return carry

    lax.fori_loop(0, 8, send_seg, 0)
    loads[7].wait()
    v_wide[...] = v_raw[...].astype(F32).reshape(TOK * 8, HD)

    def send_v(t, carry):
        j = turns(t)
        kv_buf[1, j] = v_wide[pl.ds(j, TOK, stride=8), :].astype(BF16)
        send(part_of(1, j, 1), j, 1)
        return carry

    lax.fori_loop(0, 8, send_v, 0)
    loads[8].wait()
    g_wide[...] = g_raw[...].astype(F32).reshape(TOK * 16, HD)

    def send_g(t, carry):
        j = turns(t)
        for r in range(2):
            h = 2 * j + r
            g_buf[h] = g_wide[pl.ds(h, TOK, stride=16), :].astype(BF16)
            send(part_of(0, j, r), j, r)
        return carry

    lax.fori_loop(0, 8, send_g, 0)

    def passing(kind, t):
        return pltpu.make_async_remote_copy(
            src_ref=kv_all.at[kind, t], dst_ref=kv_all.at[kind, t],
            send_sem=pass_send, recv_sem=pass_recv,
            device_id=mate_at, device_id_type=MESH,
        )

    def wait_on(ref, sem):
        pltpu.make_async_copy(ref, ref, sem).wait()

    def forward(i, carry):
        t = lax.rem(2 * (j_own + SEQ // 2 - lax.div(i, 2)) + lax.rem(i, 2), SEQ)
        wait_on(kv_all.at[core, t], pass_got.at[t])
        passing(core, t).start()
        return carry

    def tables(t, carry):
        cb, sb = block_rope(near_ref, far_ref, t)
        cos_all[t] = cb
        sin_all[t] = sb
        return carry

    lax.fori_loop(0, SEQ, tables, 0)

    @pl.when(core == 0)
    def _():
        lax.fori_loop(0, SEQ, forward, 0)

    wait_on(q_all, recv_sem.at[2])
    wait_on(seg_all, recv_sem.at[3])

    @pl.when(core == 1)
    def _():
        wait_on(kv_all.at[0], pass_recv)

    seg = seg_all[...].reshape(SEQ, TOK)
    first = jnp.zeros((SEQ, TOK), F32)
    for d in range(1, 8):
        below = jnp.where(seg < d, 1.0, 0.0)
        count = jnp.sum(jnp.sum(below, axis=1, keepdims=True), axis=0, keepdims=True)
        first = jnp.where(seg == d, count, first)
    first_ref[...] = first.astype(jnp.int32).reshape(SEQ, 1, TOK)
    gain_acc[...] = jnp.zeros_like(gain_acc)
    last = (((1,), (1,)), ((), ()))
    lead = (((0,), (0,)), ((), ()))

    def pair(ref, qi):
        return ref[pl.ds(2 * qi, 2)].reshape(BLK, HD)

    def keys_of(kind, kb):
        return kv_all[kind, pl.ds(2 * kb, 2)].reshape(BLK, HD)

    def fold(x):
        return jnp.sum(x.reshape(BLK // 8, 8, BLK), axis=0)

    def by_queries(qi, run):
        for count in range(1, BAND + 1):
            fits = (qi >= BAND - 1) if count == BAND else (qi == count - 1)

            @pl.when(fits)
            def _(count=count):
                run(qi, count)

    def by_keys(i, run):
        kb = turns(i)
        for count in range(1, BAND + 1):
            fits = (kb <= NBLK - BAND) if count == BAND else (kb == NBLK - count)

            @pl.when(fits)
            def _(count=count):
                run(kb, count)

    def forward_block(qi, count):
        queries = pair(q_all, qi)
        firsts = jnp.concatenate([first_ref[2 * qi], first_ref[2 * qi + 1]], axis=1)
        key_at = lax.broadcasted_iota(jnp.int32, (BLK, BLK), 0)
        query_at = lax.broadcasted_iota(jnp.int32, (BLK, BLK), 1)
        total = jnp.zeros((8, BLK), F32)
        for d in range(count):
            st = lax.dot_general(keys_of(0, qi - d), queries, last, preferred_element_type=F32)
            seen = key_at >= firsts - (qi - d) * BLK
            if d == 0:
                seen = seen & (key_at <= query_at)
            e = jnp.where(seen, jnp.exp2(st), 0.0)
            expo[d] = e
            total = total + fold(e)
        inv = 1.0 / jnp.sum(total, axis=0, keepdims=True)
        for d in range(count):
            prob[qi, d] = (expo[d] * inv).astype(BF16)

    def forward_step(i, carry):
        by_queries(turns(i), forward_block)

        @pl.when(core == 1)
        def _():
            forward(2 * i, 0)
            forward(2 * i + 1, 0)

        return carry

    lax.fori_loop(0, NBLK, forward_step, 0)

    def units(t, carry):
        cb, sb = cos_all[t], sin_all[t]
        q_unit[t] = turn_back(q_all[t].astype(F32), cb, sb)
        k_unit[t] = turn_back(kv_all[0, t].astype(F32), cb, sb)
        return carry

    lax.fori_loop(0, SEQ, units, 0)

    @pl.when(core == 0)
    def _():
        wait_on(kv_all.at[1], pass_recv)

    def swap(kind, t):
        return pltpu.make_async_remote_copy(
            src_ref=dkv_buf.at[kind, t], dst_ref=mate.at[t],
            send_sem=swap_send, recv_sem=swap_recv.at[t],
            device_id=mate_at, device_id_type=MESH,
        )

    slot_q = 2 * j_own + core
    slot_kv = core * 8 + j_own

    def homeward(kind, src, dst, t):
        return pltpu.make_async_remote_copy(
            src_ref=src, dst_ref=dst, send_sem=back_send.at[kind], recv_sem=back_recv.at[kind],
            device_id=(2 * z + span, t), device_id_type=MESH,
        )

    def back_part(kind, t):
        if kind == 0:
            return (0, dq_buf.at[t], dq_out.at[slot_q])
        return (1, mine.at[t], dkv_out.at[slot_kv])

    def home(t):
        return (span == core) & (t == s)

    def send_back(part, t):
        kind, src, dst = part

        @pl.when(home(t))
        def _():
            pltpu.make_async_copy(src, dst, back_recv.at[kind]).start()

        @pl.when(jnp.logical_not(home(t)))
        def _():
            homeward(kind, src, dst, t).start()

    def settle(kind, t):
        swap(kind, t).wait_recv()
        mine[t] = (dkv_buf[kind, t].astype(F32) + mate[t].astype(F32)).astype(BF16)
        send_back(back_part(1, t), t)

    def settle_pair(kind, i):
        settle(kind, 2 * turns(i))
        settle(kind, 2 * turns(i) + 1)

    def backward_block(qi, count):
        upstream = pair(g_all, qi)
        mixed = jnp.zeros((8, BLK), F32)
        for d in range(count):
            dpt = lax.dot_general(
                keys_of(1, qi - d), upstream, last, preferred_element_type=F32
            )
            pgrad[d] = dpt
            mixed = mixed + fold(prob[qi, d].astype(F32) * dpt)
        delta = jnp.sum(mixed, axis=0, keepdims=True)
        dq = jnp.zeros((BLK, HD), F32)
        for d in range(count):
            ds = (prob[qi, d].astype(F32) * (pgrad[d] - delta)).astype(BF16)
            sgrad[qi, d] = ds
            dq = dq + lax.dot_general(ds, keys_of(0, qi - d), lead, preferred_element_type=F32)
        dq_acc[...] = dq * SCALE

    def backward_step(i, carry):
        qi = lax.rem(j_own + NBLK - i, NBLK)
        for half in range(2):
            wait_on(g_all.at[2 * qi + half], g_got.at[2 * qi + half])
        by_queries(qi, backward_block)
        gain = gain_acc[...]
        for half in range(2):
            block = 2 * qi + half
            rows = dq_acc[half * TOK:(half + 1) * TOK, :]
            dq_buf[block] = rows.astype(BF16)
            send_back(back_part(0, block), block)
            both = turn_back(rows, cos_all[block], sin_all[block]) * q_unit[block]
            gain = gain + jnp.sum(both.reshape(TOK // 8, 8, HD), axis=0)
        gain_acc[...] = gain

        return carry

    lax.fori_loop(0, NBLK, backward_step, 0)

    def key_block(kb, count):
        dk = jnp.dot(sgrad[kb, 0], pair(q_all, kb), preferred_element_type=F32)
        for d in range(1, count):
            dk = dk + jnp.dot(sgrad[kb + d, d], pair(q_all, kb + d), preferred_element_type=F32)
        dq_acc[...] = dk * LN2

    def key_step(i, gain):
        by_keys(i, key_block)
        kb = turns(i)
        dkv_buf[0, pl.ds(2 * kb, 2)] = dq_acc[...].astype(BF16).reshape(2, TOK, HD)

        @pl.when(core == 1)
        def _():
            swap(0, 2 * kb).start()
            swap(0, 2 * kb + 1).start()

        for half in range(2):
            block = 2 * kb + half
            rows = dq_acc[half * TOK:(half + 1) * TOK, :]
            both = turn_back(rows, cos_all[block], sin_all[block]) * k_unit[block]
            gain = gain + jnp.sum(both.reshape(TOK // 8, 8, HD), axis=0)

        @pl.when((core == 0) & (i > 0))
        def _():
            settle_pair(0, i - 1)

        return gain

    gain_k = lax.fori_loop(0, NBLK, key_step, jnp.zeros((8, HD), F32))
    row = lax.broadcasted_iota(jnp.int32, (8, HD), 0)
    gain_one[0] = jnp.where(
        row == 0,
        jnp.sum(gain_acc[...], axis=0, keepdims=True),
        jnp.where(row == 1, jnp.sum(gain_k, axis=0, keepdims=True), 0.0),
    )

    def share(stage, i):
        return pltpu.make_async_remote_copy(
            src_ref=gain_one.at[stage], dst_ref=stages.at[stage, rank[stage]],
            send_sem=stage_send.at[stage], recv_sem=stage_recv.at[stage],
            device_id=member(stage, i), device_id_type=MESH,
        )

    def share_all(stage):
        def one(i, carry):
            @pl.when(i != rank[stage])
            def _():
                share(stage, i).start()

            return carry

        lax.fori_loop(0, sizes[stage], one, 0)
        stages[stage, rank[stage]] = gain_one[stage]

    def gathered(stage):
        wait_on(stages.at[stage, pl.ds(0, sizes[stage] - 1)], stage_recv.at[stage])
        return jnp.sum(stages[stage, 0:sizes[stage]], axis=0)

    share_all(0)

    @pl.when(core == 0)
    def _():
        settle_pair(0, NBLK - 1)

    def value_block(kb, count):
        dv = jnp.dot(prob[kb, 0], pair(g_all, kb), preferred_element_type=F32)
        for d in range(1, count):
            dv = dv + jnp.dot(prob[kb + d, d], pair(g_all, kb + d), preferred_element_type=F32)
        dkv_buf[1, pl.ds(2 * kb, 2)] = dv.astype(BF16).reshape(2, TOK, HD)

    def value_step(i, carry):
        by_keys(i, value_block)
        kb = turns(i)

        @pl.when(core == 0)
        def _():
            swap(1, 2 * kb).start()
            swap(1, 2 * kb + 1).start()

        @pl.when((core == 1) & (i > 0))
        def _():
            settle_pair(1, i - 1)

        return carry

    lax.fori_loop(0, NBLK, value_step, 0)

    @pl.when(core == 1)
    def _():
        settle_pair(1, NBLK - 1)

    gain_one[1] = gathered(0)
    share_all(1)

    def norm_back(upstream, gain, unit, size):
        slope = turn_back(upstream.astype(F32), cosine, sine) * gain
        return size * (slope - unit * jnp.mean(slope * unit, axis=1, keepdims=True))

    wait_on(dq_out, back_recv.at[0])
    for h in range(16):
        q_wide[pl.ds(h, TOK, stride=16), :] = norm_back(
            dq_out[h], qg_ref[...], q_row[h], q_size[h]
        )
    q_raw[...] = q_wide[...].reshape(TOK, 16, HD).astype(BF16)
    stores = [
        pltpu.make_async_copy(src, dst, store_sem.at[i])
        for i, (src, dst) in enumerate(
            (
                (q_raw, gq_out), (k_raw, gk_out), (v_raw, gv_out),
                (gain_two.at[0], gqg_out), (gain_two.at[1], gkg_out),
            )
        )
    ]
    stores[0].start()
    wait_on(dkv_out, back_recv.at[1])
    for j in range(8):
        k_wide[pl.ds(j, TOK, stride=8), :] = norm_back(
            dkv_out[j], kg_ref[...], k_row[j], k_size[j]
        )
    k_raw[...] = k_wide[...].reshape(TOK, 8, HD).astype(BF16)
    stores[1].start()
    for j in range(8):
        v_wide[pl.ds(j, TOK, stride=8), :] = dkv_out[8 + j].astype(F32)
    v_raw[...] = v_wide[...].reshape(TOK, 8, HD).astype(BF16)
    stores[2].start()
    wait_on(kv_all.at[0], pass_send)
    wait_on(mate, swap_send)
    wait_on(stages.at[0, pl.ds(0, 15)], stage_send.at[0])
    near_one = span == core

    @pl.when(near_one)
    def _():
        few = pl.ds(0, SEQ - 1)
        wait_on(g_buf.at[few], send_sem.at[0])
        wait_on(q_buf.at[few], send_sem.at[2])
        wait_on(seg_all.at[few], send_sem.at[3])
        wait_on(g_buf.at[few], send_sem.at[1])
        wait_on(dq_buf.at[few], back_send.at[0])
        wait_on(mine.at[few], back_send.at[1])

    @pl.when(jnp.logical_not(near_one))
    def _():
        wait_on(g_buf, send_sem.at[0])
        wait_on(q_buf, send_sem.at[2])
        wait_on(seg_all, send_sem.at[3])
        wait_on(g_buf, send_sem.at[1])
        wait_on(dq_buf, back_send.at[0])
        wait_on(mine, back_send.at[1])

    wait_on(stages.at[1, pl.ds(0, 31)], stage_send.at[1])
    total = gathered(1)
    gain_two[0] = total[0:1, :] / (qg_ref[...] * QMUL)
    gain_two[1] = total[1:2, :] / kg_ref[...]
    stores[3].start()
    stores[4].start()
    for copy in stores:
        copy.wait()


def store_kernel(q_ref, k_ref, v_ref, qg_ref, kg_ref, q_to, k_to, v_to, qg_to, kg_to):
    q_to[...] = q_ref[...]
    k_to[...] = k_ref[...]
    v_to[...] = v_ref[...]
    qg_to[...] = qg_ref[...]
    kg_to[...] = kg_ref[...]


def shape(dims, dtype):
    return jax.ShapeDtypeStruct(dims, dtype)


def body(q_pre, k_pre, values, grad_out, segment_ids, q_gain, k_gain):
    near, far = (jnp.asarray(table) for table in rope_tables())
    qg, kg = q_gain.reshape(1, HD), k_gain.reshape(1, HD)
    dma = pltpu.SemaphoreType.DMA
    tiles = (SEQ, TOK, HD)
    kinds = (
        shape((TOK, 16, HD), BF16), shape((TOK, 8, HD), BF16), shape((TOK, 8, HD), BF16),
        shape((1, HD), F32), shape((1, HD), F32),
    )
    results = pl.pallas_call(
        fused_kernel,
        name="heads_and_back",
        out_shape=kinds,
        in_specs=[HBM] * 9,
        out_specs=(ANY,) * 5,
        scratch_shapes=[
            pltpu.VMEM((TOK, 16, HD), BF16), pltpu.VMEM((TOK, 8, HD), BF16),
            pltpu.VMEM((TOK, 8, HD), BF16), pltpu.VMEM((TOK, 16, HD), BF16),
            pltpu.VMEM((1, TOK), jnp.int32), pltpu.VMEM((1, HD), F32), pltpu.VMEM((1, HD), F32),
            pltpu.VMEM((2, TOK, HD), F32), pltpu.VMEM((SEQ, 2, HD), F32),
            pltpu.VMEM((TOK * 16, HD), F32), pltpu.VMEM((TOK * 8, HD), F32),
            pltpu.VMEM((TOK * 8, HD), F32), pltpu.VMEM((TOK * 16, HD), F32),
            pltpu.VMEM(tiles, F32), pltpu.VMEM((8, TOK, HD), F32),
            pltpu.VMEM(tiles, F32), pltpu.VMEM((8, TOK, HD), F32),
            pltpu.VMEM(tiles, BF16), pltpu.VMEM(tiles, BF16),
            pltpu.VMEM((2, 8, TOK, HD), BF16),
            pltpu.VMEM(tiles, BF16), pltpu.VMEM(tiles, BF16), pltpu.VMEM((2,) + tiles, BF16),
            pltpu.VMEM((SEQ, 1, TOK), jnp.int32), pltpu.VMEM((SEQ, 1, TOK), jnp.int32),
            pltpu.VMEM(tiles, F32), pltpu.VMEM(tiles, F32),
            pltpu.VMEM(tiles, F32), pltpu.VMEM(tiles, F32),
            pltpu.VMEM((BAND, BLK, BLK), F32), pltpu.VMEM((NBLK, BAND, BLK, BLK), BF16),
            pltpu.VMEM((NBLK, BAND, BLK, BLK), BF16),
            pltpu.VMEM((BAND, BLK, BLK), F32), pltpu.VMEM((BLK, HD), F32),
            pltpu.VMEM((8, HD), F32),
            pltpu.VMEM(tiles, BF16), pltpu.VMEM((2,) + tiles, BF16),
            pltpu.VMEM(tiles, BF16), pltpu.VMEM(tiles, BF16),
            pltpu.VMEM(tiles, BF16), pltpu.VMEM(tiles, BF16),
            pltpu.VMEM((2, 8, HD), F32), pltpu.VMEM((2, 32, 8, HD), F32),
            pltpu.VMEM((2, 1, HD), F32),
            dma((9,)), dma((4,)), dma((4,)), dma, dma, dma((SEQ,)), dma((SEQ,)),
            dma((2,)), dma((2,)), dma, dma((SEQ,)), dma((2,)), dma((2,)), dma((5,)),
        ],
        compiler_params=pltpu.CompilerParams(
            collective_id=0, has_side_effects=True, vmem_limit_bytes=48 << 20
        ),
    )(*(
        pltpu.with_memory_space_constraint(x, pltpu.HBM)
        for x in (
            q_pre[0], k_pre[0], values[0], grad_out[0], segment_ids, qg, kg, near, far
        )
    ))

    grad_q, grad_k, grad_v, grad_qg, grad_kg = pl.pallas_call(
        store_kernel,
        name="store_results",
        out_shape=kinds,
        in_specs=[pl.BlockSpec(memory_space=pltpu.VMEM)] * 5,
        out_specs=(pl.BlockSpec(memory_space=pltpu.VMEM),) * 5,
        compiler_params=pltpu.CompilerParams(vmem_limit_bytes=32 << 20),
    )(*results)
    return (
        grad_q[None], grad_k[None], grad_v[None], grad_qg.reshape(HD), grad_kg.reshape(HD)
    )


def solution(mesh):
    tokens = P("dp", "seq", None, None)
    return jax.shard_map(
        body,
        mesh=mesh,
        in_specs=(tokens, tokens, tokens, tokens, P("dp", "seq"), P(), P()),
        out_specs=(tokens, tokens, tokens, P(), P()),
        check_vma=False,
    )
```

```python
import jax
import jax.numpy as jnp
import numpy as np
from jax import lax
from jax.experimental import pallas as pl
from jax.experimental.pallas import tpu as pltpu
from jax.sharding import PartitionSpec as P

PRESCALE = 168
HD = 128
SEQ = 16
TOK = 128
TOTAL = SEQ * TOK
BLK = 256
NBLK = TOTAL // BLK
BAND = 5
EPS = 1e-6
ROPE_BASE = 1000000.0
ROPE_FACTOR = 8.0
SCALE = float(PRESCALE) ** (-0.5)
QMUL = SCALE * float(np.log2(np.e))
LN2 = float(np.log(2.0))
MESH = pl.DeviceIdType.MESH
F32 = jnp.float32
BF16 = jnp.bfloat16
ANY = pl.BlockSpec(memory_space=pl.ANY)
HBM = pl.BlockSpec(memory_space=pltpu.HBM)


def rope_tables():
    half = HD // 2
    freqs = ROPE_BASE ** (-(np.arange(half, dtype=np.float64) * 2.0 / HD))
    freqs = np.concatenate([freqs, freqs])
    near = np.arange(TOK, dtype=np.float64)[:, None] / ROPE_FACTOR * freqs[None, :]
    far = np.arange(SEQ, dtype=np.float64)[:, None] * TOK / ROPE_FACTOR * freqs[None, :]
    return (
        np.stack([np.cos(near), np.sin(near)]).astype(np.float32),
        np.stack([np.cos(far), np.sin(far)], axis=1).astype(np.float32),
    )


def block_rope(near_ref, far_ref, block):
    far = far_ref[block]
    cb, sb = far[0:1, :], far[1:2, :]
    cosine = near_ref[0] * cb - near_ref[1] * sb
    sine = near_ref[1] * cb + near_ref[0] * sb
    lane = lax.broadcasted_iota(jnp.int32, (TOK, HD), 1)
    return cosine, jnp.where(lane < HD // 2, -sine, sine)


def turn(rows, cosine, sine):
    return rows * cosine + pltpu.roll(rows, HD // 2, 1) * sine


def turn_back(rows, cosine, sine):
    return rows * cosine - pltpu.roll(rows, HD // 2, 1) * sine


def place():
    dp = lax.axis_index("dp")
    s = lax.axis_index("seq")
    z = lax.div(dp, 2)
    return dp, s, z, lax.rem(dp, 2)


def fused_kernel(
    q_hbm, k_hbm, v_hbm, g_hbm, seg_hbm, qg_hbm, kg_hbm, near_hbm, far_hbm,
    gq_out, gk_out, gv_out, gqg_out, gkg_out,
    q_raw, k_raw, v_raw, g_raw, seg_one, qg_ref, kg_ref, near_ref, far_ref,
    q_wide, k_wide, v_wide, g_wide, q_row, k_row, q_size, k_size, q_buf, g_buf, kv_buf,
    q_all, g_all, kv_all, seg_all, first_ref, cos_all, sin_all, q_unit, k_unit,
    expo, prob, sgrad, pgrad, dq_acc, gain_acc,
    dq_buf, dkv_buf, mate, mine, dq_out, dkv_out, gain_one, stages, gain_two,
    load_sem, send_sem, recv_sem, pass_send, pass_recv, pass_got, g_got, q_got,
    back_send, back_recv, swap_send, swap_recv, stage_send, stage_recv, store_sem,
):
    dp, s, z, core = place()
    j_own = lax.div(s, 2)
    span = lax.rem(s, 2)
    mate_at = (2 * z + 1 - core, s)
    loads = [
        pltpu.make_async_copy(src, dst, load_sem.at[i])
        for i, (src, dst) in enumerate(
            (
                (k_hbm, k_raw), (near_hbm, near_ref), (far_hbm, far_ref), (kg_hbm, kg_ref),
                (qg_hbm, qg_ref), (seg_hbm, seg_one), (q_hbm, q_raw), (v_hbm, v_raw),
                (g_hbm, g_raw),
            )
        )
    ]
    for copy in loads:
        copy.start()
    barrier = pltpu.get_barrier_semaphore()

    def greet(i, carry):
        @pl.when(i != core * SEQ + s)
        def _():
            pl.semaphore_signal(
                barrier, inc=1, device_id=(2 * z + lax.div(i, SEQ), lax.rem(i, SEQ)),
                device_id_type=MESH,
            )

        return carry

    sizes = (16, 32)
    rank = (z, core * SEQ + s)

    def member(stage, i):
        if stage == 0:
            return (2 * i + core, s)
        return (2 * z + lax.div(i, SEQ), lax.rem(i, SEQ))

    def greet_z(i, carry):
        @pl.when(i != z)
        def _():
            pl.semaphore_signal(barrier, inc=1, device_id=member(0, i), device_id_type=MESH)

        return carry

    lax.fori_loop(0, 2 * SEQ, greet, 0)
    lax.fori_loop(0, 16, greet_z, 0)
    for copy in loads[:6]:
        copy.wait()
    cosine, sine = block_rope(near_ref, far_ref, s)
    k_wide[...] = k_raw[...].astype(F32).reshape(TOK * 8, HD)

    def prepare(wide, rows_at, gain, row, size_at):
        rows = wide[rows_at, :]
        size = lax.rsqrt(jnp.mean(rows * rows, axis=1, keepdims=True) + EPS)
        unit = rows * size
        row[...] = unit
        size_at[...] = jnp.broadcast_to(size, (TOK, HD))
        return turn(unit * gain, cosine, sine)

    for j in range(8):
        kv_buf[0, j] = prepare(
            k_wide, pl.ds(j, TOK, stride=8), kg_ref[...], k_row.at[j], k_size.at[j]
        ).astype(BF16)
    pl.semaphore_wait(barrier, 2 * SEQ - 1 + 15)

    def is_me(j, r):
        return (2 * z + r == dp) & (2 * j + core == s)

    def landing(kind):
        if kind == 0:
            return g_got.at[s]
        if kind == 2:
            return q_got.at[s]
        return recv_sem.at[kind] if kind != 1 else pass_got.at[s]

    def outward(kind, src, dst, j, r):
        return pltpu.make_async_remote_copy(
            src_ref=src, dst_ref=dst, send_sem=send_sem.at[kind], recv_sem=landing(kind),
            device_id=(2 * z + r, 2 * j + core), device_id_type=MESH,
        )

    def send(part, j, r):
        kind, src, dst = part
        me = is_me(j, r)

        @pl.when(me)
        def _():
            pltpu.make_async_copy(src, dst, landing(kind)).start()

        @pl.when(jnp.logical_not(me))
        def _():
            outward(kind, src, dst, j, r).start()

    def part_of(kind, j, r):
        h = 2 * j + r
        if kind == 0:
            return (0, g_buf.at[h], g_all.at[s])
        if kind == 1:
            return (1, kv_buf.at[r, j], kv_all.at[r, s])
        if kind == 2:
            return (2, q_buf.at[h], q_all.at[s])
        return (3, seg_one, seg_all.at[s])

    def turns(t):
        return lax.rem(j_own + t, SEQ // 2)

    def send_k(t, carry):
        j = turns(t)
        send(part_of(1, j, 0), j, 0)
        return carry

    lax.fori_loop(0, 8, send_k, 0)

    def send_seg(t, carry):
        j = turns(t)
        for r in range(2):
            send(part_of(3, j, r), j, r)
        return carry

    lax.fori_loop(0, 8, send_seg, 0)
    loads[6].wait()
    q_wide[...] = q_raw[...].astype(F32).reshape(TOK * 16, HD)

    def send_q(t, carry):
        j = turns(t)
        for r in range(2):
            h = 2 * j + r
            q_buf[h] = (prepare(
                q_wide, pl.ds(h, TOK, stride=16), qg_ref[...], q_row.at[h], q_size.at[h]
            ) * QMUL).astype(BF16)
            send(part_of(2, j, r), j, r)
        return carry

    lax.fori_loop(0, 8, send_q, 0)

    loads[7].wait()
    v_wide[...] = v_raw[...].astype(F32).reshape(TOK * 8, HD)

    def send_v(t, carry):
        j = turns(t)
        kv_buf[1, j] = v_wide[pl.ds(j, TOK, stride=8), :].astype(BF16)
        send(part_of(1, j, 1), j, 1)
        return carry

    lax.fori_loop(0, 8, send_v, 0)
    loads[8].wait()
    g_wide[...] = g_raw[...].astype(F32).reshape(TOK * 16, HD)

    def send_g(t, carry):
        j = turns(t)
        for r in range(2):
            h = 2 * j + r
            g_buf[h] = g_wide[pl.ds(h, TOK, stride=16), :].astype(BF16)
            send(part_of(0, j, r), j, r)
        return carry

    lax.fori_loop(0, 8, send_g, 0)

    def passing(kind, t):
        return pltpu.make_async_remote_copy(
            src_ref=kv_all.at[kind, t], dst_ref=kv_all.at[kind, t],
            send_sem=pass_send, recv_sem=pass_recv,
            device_id=mate_at, device_id_type=MESH,
        )

    def wait_on(ref, sem):
        pltpu.make_async_copy(ref, ref, sem).wait()

    def forward(i, carry):
        t = lax.rem(2 * (j_own + SEQ // 2 - lax.div(i, 2)) + lax.rem(i, 2), SEQ)
        wait_on(kv_all.at[core, t], pass_got.at[t])
        passing(core, t).start()
        return carry

    def tables(t, carry):
        cb, sb = block_rope(near_ref, far_ref, t)
        cos_all[t] = cb
        sin_all[t] = sb
        return carry

    lax.fori_loop(0, SEQ, tables, 0)

    @pl.when(core == 0)
    def _():
        lax.fori_loop(0, SEQ, forward, 0)

    wait_on(seg_all, recv_sem.at[3])

    @pl.when(core == 1)
    def _():
        wait_on(kv_all.at[0], pass_recv)

    seg = seg_all[...].reshape(SEQ, TOK)
    first = jnp.zeros((SEQ, TOK), F32)
    for d in range(1, 8):
        below = jnp.where(seg < d, 1.0, 0.0)
        count = jnp.sum(jnp.sum(below, axis=1, keepdims=True), axis=0, keepdims=True)
        first = jnp.where(seg == d, count, first)
    first_ref[...] = first.astype(jnp.int32).reshape(SEQ, 1, TOK)
    gain_acc[...] = jnp.zeros_like(gain_acc)
    last = (((1,), (1,)), ((), ()))
    lead = (((0,), (0,)), ((), ()))

    def pair(ref, qi):
        return ref[pl.ds(2 * qi, 2)].reshape(BLK, HD)

    def keys_of(kind, kb):
        return kv_all[kind, pl.ds(2 * kb, 2)].reshape(BLK, HD)

    def fold(x):
        return jnp.sum(x.reshape(BLK // 8, 8, BLK), axis=0)

    def by_queries(qi, run):
        for count in range(1, BAND + 1):
            fits = (qi >= BAND - 1) if count == BAND else (qi == count - 1)

            @pl.when(fits)
            def _(count=count):
                run(qi, count)

    def by_keys(i, run):
        kb = turns(i)
        for count in range(1, BAND + 1):
            fits = (kb <= NBLK - BAND) if count == BAND else (kb == NBLK - count)

            @pl.when(fits)
            def _(count=count):
                run(kb, count)

    def forward_block(qi, count):
        queries = pair(q_all, qi)
        firsts = jnp.concatenate([first_ref[2 * qi], first_ref[2 * qi + 1]], axis=1)
        key_at = lax.broadcasted_iota(jnp.int32, (BLK, BLK), 0)
        query_at = lax.broadcasted_iota(jnp.int32, (BLK, BLK), 1)
        total = jnp.zeros((8, BLK), F32)
        for d in range(count):
            st = lax.dot_general(keys_of(0, qi - d), queries, last, preferred_element_type=F32)
            seen = key_at >= firsts - (qi - d) * BLK
            if d == 0:
                seen = seen & (key_at <= query_at)
            e = jnp.where(seen, jnp.exp2(st), 0.0)
            expo[d] = e
            total = total + fold(e)
        inv = 1.0 / jnp.sum(total, axis=0, keepdims=True)
        for d in range(count):
            prob[qi, d] = (expo[d] * inv).astype(BF16)

    def forward_step(i, carry):
        qi = lax.rem(j_own + NBLK - i, NBLK)
        for half in range(2):
            wait_on(q_all.at[2 * qi + half], q_got.at[2 * qi + half])
        by_queries(qi, forward_block)
        return carry

    lax.fori_loop(0, NBLK, forward_step, 0)

    def units(t, carry):
        cb, sb = cos_all[t], sin_all[t]
        q_unit[t] = turn_back(q_all[t].astype(F32), cb, sb)
        k_unit[t] = turn_back(kv_all[0, t].astype(F32), cb, sb)
        return carry

    lax.fori_loop(0, SEQ, units, 0)

    @pl.when(core == 1)
    def _():
        lax.fori_loop(0, SEQ, forward, 0)


    @pl.when(core == 0)
    def _():
        wait_on(kv_all.at[1], pass_recv)

    def swap(kind, t):
        return pltpu.make_async_remote_copy(
            src_ref=dkv_buf.at[kind, t], dst_ref=mate.at[t],
            send_sem=swap_send, recv_sem=swap_recv.at[t],
            device_id=mate_at, device_id_type=MESH,
        )

    slot_q = 2 * j_own + core
    slot_kv = core * 8 + j_own

    def homeward(kind, src, dst, t):
        return pltpu.make_async_remote_copy(
            src_ref=src, dst_ref=dst, send_sem=back_send.at[kind], recv_sem=back_recv.at[kind],
            device_id=(2 * z + span, t), device_id_type=MESH,
        )

    def back_part(kind, t):
        if kind == 0:
            return (0, dq_buf.at[t], dq_out.at[slot_q])
        return (1, mine.at[t], dkv_out.at[slot_kv])

    def home(t):
        return (span == core) & (t == s)

    def send_back(part, t):
        kind, src, dst = part

        @pl.when(home(t))
        def _():
            pltpu.make_async_copy(src, dst, back_recv.at[kind]).start()

        @pl.when(jnp.logical_not(home(t)))
        def _():
            homeward(kind, src, dst, t).start()

    def settle(kind, t):
        swap(kind, t).wait_recv()
        mine[t] = (dkv_buf[kind, t].astype(F32) + mate[t].astype(F32)).astype(BF16)
        send_back(back_part(1, t), t)

    def settle_pair(kind, i):
        settle(kind, 2 * turns(i))
        settle(kind, 2 * turns(i) + 1)

    def backward_block(qi, count):
        upstream = pair(g_all, qi)
        mixed = jnp.zeros((8, BLK), F32)
        for d in range(count):
            dpt = lax.dot_general(
                keys_of(1, qi - d), upstream, last, preferred_element_type=F32
            )
            pgrad[d] = dpt
            mixed = mixed + fold(prob[qi, d].astype(F32) * dpt)
        delta = jnp.sum(mixed, axis=0, keepdims=True)
        dq = jnp.zeros((BLK, HD), F32)
        for d in range(count):
            ds = (prob[qi, d].astype(F32) * (pgrad[d] - delta)).astype(BF16)
            sgrad[qi, d] = ds
            dq = dq + lax.dot_general(ds, keys_of(0, qi - d), lead, preferred_element_type=F32)
        dq_acc[...] = dq * SCALE

    def backward_step(i, carry):
        qi = lax.rem(j_own + NBLK - i, NBLK)
        for half in range(2):
            wait_on(g_all.at[2 * qi + half], g_got.at[2 * qi + half])
        by_queries(qi, backward_block)
        gain = gain_acc[...]
        for half in range(2):
            block = 2 * qi + half
            rows = dq_acc[half * TOK:(half + 1) * TOK, :]
            dq_buf[block] = rows.astype(BF16)
            send_back(back_part(0, block), block)
            both = turn_back(rows, cos_all[block], sin_all[block]) * q_unit[block]
            gain = gain + jnp.sum(both.reshape(TOK // 8, 8, HD), axis=0)
        gain_acc[...] = gain

        return carry

    lax.fori_loop(0, NBLK, backward_step, 0)

    def key_block(kb, count):
        dk = jnp.dot(sgrad[kb, 0], pair(q_all, kb), preferred_element_type=F32)
        for d in range(1, count):
            dk = dk + jnp.dot(sgrad[kb + d, d], pair(q_all, kb + d), preferred_element_type=F32)
        dq_acc[...] = dk * LN2

    def key_step(i, gain):
        by_keys(i, key_block)
        kb = turns(i)
        dkv_buf[0, pl.ds(2 * kb, 2)] = dq_acc[...].astype(BF16).reshape(2, TOK, HD)

        @pl.when(core == 1)
        def _():
            swap(0, 2 * kb).start()
            swap(0, 2 * kb + 1).start()

        for half in range(2):
            block = 2 * kb + half
            rows = dq_acc[half * TOK:(half + 1) * TOK, :]
            both = turn_back(rows, cos_all[block], sin_all[block]) * k_unit[block]
            gain = gain + jnp.sum(both.reshape(TOK // 8, 8, HD), axis=0)

        @pl.when((core == 0) & (i > 0))
        def _():
            settle_pair(0, i - 1)

        return gain

    gain_k = lax.fori_loop(0, NBLK, key_step, jnp.zeros((8, HD), F32))
    row = lax.broadcasted_iota(jnp.int32, (8, HD), 0)
    gain_one[0] = jnp.where(
        row == 0,
        jnp.sum(gain_acc[...], axis=0, keepdims=True),
        jnp.where(row == 1, jnp.sum(gain_k, axis=0, keepdims=True), 0.0),
    )

    def share(stage, i):
        return pltpu.make_async_remote_copy(
            src_ref=gain_one.at[stage], dst_ref=stages.at[stage, rank[stage]],
            send_sem=stage_send.at[stage], recv_sem=stage_recv.at[stage],
            device_id=member(stage, i), device_id_type=MESH,
        )

    def share_all(stage):
        def one(i, carry):
            @pl.when(i != rank[stage])
            def _():
                share(stage, i).start()

            return carry

        lax.fori_loop(0, sizes[stage], one, 0)
        stages[stage, rank[stage]] = gain_one[stage]

    def gathered(stage):
        wait_on(stages.at[stage, pl.ds(0, sizes[stage] - 1)], stage_recv.at[stage])
        return jnp.sum(stages[stage, 0:sizes[stage]], axis=0)

    share_all(0)

    @pl.when(core == 0)
    def _():
        settle_pair(0, NBLK - 1)

    def value_block(kb, count):
        dv = jnp.dot(prob[kb, 0], pair(g_all, kb), preferred_element_type=F32)
        for d in range(1, count):
            dv = dv + jnp.dot(prob[kb + d, d], pair(g_all, kb + d), preferred_element_type=F32)
        dkv_buf[1, pl.ds(2 * kb, 2)] = dv.astype(BF16).reshape(2, TOK, HD)

    def value_step(i, carry):
        by_keys(i, value_block)
        kb = turns(i)

        @pl.when(core == 0)
        def _():
            swap(1, 2 * kb).start()
            swap(1, 2 * kb + 1).start()

        @pl.when((core == 1) & (i > 0))
        def _():
            settle_pair(1, i - 1)

        return carry

    lax.fori_loop(0, NBLK, value_step, 0)

    @pl.when(core == 1)
    def _():
        settle_pair(1, NBLK - 1)

    gain_one[1] = gathered(0)
    share_all(1)

    def norm_back(upstream, gain, unit, size):
        slope = turn_back(upstream.astype(F32), cosine, sine) * gain
        return size * (slope - unit * jnp.mean(slope * unit, axis=1, keepdims=True))

    wait_on(dq_out, back_recv.at[0])
    for h in range(16):
        q_wide[pl.ds(h, TOK, stride=16), :] = norm_back(
            dq_out[h], qg_ref[...], q_row[h], q_size[h]
        )
    q_raw[...] = q_wide[...].reshape(TOK, 16, HD).astype(BF16)
    stores = [
        pltpu.make_async_copy(src, dst, store_sem.at[i])
        for i, (src, dst) in enumerate(
            (
                (q_raw, gq_out), (k_raw, gk_out), (v_raw, gv_out),
                (gain_two.at[0], gqg_out), (gain_two.at[1], gkg_out),
            )
        )
    ]
    stores[0].start()
    wait_on(dkv_out, back_recv.at[1])
    for j in range(8):
        k_wide[pl.ds(j, TOK, stride=8), :] = norm_back(
            dkv_out[j], kg_ref[...], k_row[j], k_size[j]
        )
    k_raw[...] = k_wide[...].reshape(TOK, 8, HD).astype(BF16)
    stores[1].start()
    for j in range(8):
        v_wide[pl.ds(j, TOK, stride=8), :] = dkv_out[8 + j].astype(F32)
    v_raw[...] = v_wide[...].reshape(TOK, 8, HD).astype(BF16)
    stores[2].start()
    wait_on(kv_all.at[0], pass_send)
    wait_on(mate, swap_send)
    wait_on(stages.at[0, pl.ds(0, 15)], stage_send.at[0])
    near_one = span == core

    @pl.when(near_one)
    def _():
        few = pl.ds(0, SEQ - 1)
        wait_on(g_buf.at[few], send_sem.at[0])
        wait_on(q_buf.at[few], send_sem.at[2])
        wait_on(seg_all.at[few], send_sem.at[3])
        wait_on(g_buf.at[few], send_sem.at[1])
        wait_on(dq_buf.at[few], back_send.at[0])
        wait_on(mine.at[few], back_send.at[1])

    @pl.when(jnp.logical_not(near_one))
    def _():
        wait_on(g_buf, send_sem.at[0])
        wait_on(q_buf, send_sem.at[2])
        wait_on(seg_all, send_sem.at[3])
        wait_on(g_buf, send_sem.at[1])
        wait_on(dq_buf, back_send.at[0])
        wait_on(mine, back_send.at[1])

    wait_on(stages.at[1, pl.ds(0, 31)], stage_send.at[1])
    total = gathered(1)
    gain_two[0] = total[0:1, :] / (qg_ref[...] * QMUL)
    gain_two[1] = total[1:2, :] / kg_ref[...]
    stores[3].start()
    stores[4].start()
    for copy in stores:
        copy.wait()


def store_kernel(q_ref, k_ref, v_ref, qg_ref, kg_ref, q_to, k_to, v_to, qg_to, kg_to):
    q_to[...] = q_ref[...]
    k_to[...] = k_ref[...]
    v_to[...] = v_ref[...]
    qg_to[...] = qg_ref[...]
    kg_to[...] = kg_ref[...]


def shape(dims, dtype):
    return jax.ShapeDtypeStruct(dims, dtype)


def body(q_pre, k_pre, values, grad_out, segment_ids, q_gain, k_gain):
    near, far = (jnp.asarray(table) for table in rope_tables())
    qg, kg = q_gain.reshape(1, HD), k_gain.reshape(1, HD)
    dma = pltpu.SemaphoreType.DMA
    tiles = (SEQ, TOK, HD)
    kinds = (
        shape((TOK, 16, HD), BF16), shape((TOK, 8, HD), BF16), shape((TOK, 8, HD), BF16),
        shape((1, HD), F32), shape((1, HD), F32),
    )
    results = pl.pallas_call(
        fused_kernel,
        name="heads_and_back",
        out_shape=kinds,
        in_specs=[HBM] * 9,
        out_specs=(ANY,) * 5,
        scratch_shapes=[
            pltpu.VMEM((TOK, 16, HD), BF16), pltpu.VMEM((TOK, 8, HD), BF16),
            pltpu.VMEM((TOK, 8, HD), BF16), pltpu.VMEM((TOK, 16, HD), BF16),
            pltpu.VMEM((1, TOK), jnp.int32), pltpu.VMEM((1, HD), F32), pltpu.VMEM((1, HD), F32),
            pltpu.VMEM((2, TOK, HD), F32), pltpu.VMEM((SEQ, 2, HD), F32),
            pltpu.VMEM((TOK * 16, HD), F32), pltpu.VMEM((TOK * 8, HD), F32),
            pltpu.VMEM((TOK * 8, HD), F32), pltpu.VMEM((TOK * 16, HD), F32),
            pltpu.VMEM(tiles, F32), pltpu.VMEM((8, TOK, HD), F32),
            pltpu.VMEM(tiles, F32), pltpu.VMEM((8, TOK, HD), F32),
            pltpu.VMEM(tiles, BF16), pltpu.VMEM(tiles, BF16),
            pltpu.VMEM((2, 8, TOK, HD), BF16),
            pltpu.VMEM(tiles, BF16), pltpu.VMEM(tiles, BF16), pltpu.VMEM((2,) + tiles, BF16),
            pltpu.VMEM((SEQ, 1, TOK), jnp.int32), pltpu.VMEM((SEQ, 1, TOK), jnp.int32),
            pltpu.VMEM(tiles, F32), pltpu.VMEM(tiles, F32),
            pltpu.VMEM(tiles, F32), pltpu.VMEM(tiles, F32),
            pltpu.VMEM((BAND, BLK, BLK), F32), pltpu.VMEM((NBLK, BAND, BLK, BLK), BF16),
            pltpu.VMEM((NBLK, BAND, BLK, BLK), BF16),
            pltpu.VMEM((BAND, BLK, BLK), F32), pltpu.VMEM((BLK, HD), F32),
            pltpu.VMEM((8, HD), F32),
            pltpu.VMEM(tiles, BF16), pltpu.VMEM((2,) + tiles, BF16),
            pltpu.VMEM(tiles, BF16), pltpu.VMEM(tiles, BF16),
            pltpu.VMEM(tiles, BF16), pltpu.VMEM(tiles, BF16),
            pltpu.VMEM((2, 8, HD), F32), pltpu.VMEM((2, 32, 8, HD), F32),
            pltpu.VMEM((2, 1, HD), F32),
            dma((9,)), dma((4,)), dma((4,)), dma, dma, dma((SEQ,)), dma((SEQ,)), dma((SEQ,)),
            dma((2,)), dma((2,)), dma, dma((SEQ,)), dma((2,)), dma((2,)), dma((5,)),
        ],
        compiler_params=pltpu.CompilerParams(
            collective_id=0, has_side_effects=True, vmem_limit_bytes=48 << 20
        ),
    )(*(
        pltpu.with_memory_space_constraint(x, pltpu.HBM)
        for x in (
            q_pre[0], k_pre[0], values[0], grad_out[0], segment_ids, qg, kg, near, far
        )
    ))

    grad_q, grad_k, grad_v, grad_qg, grad_kg = pl.pallas_call(
        store_kernel,
        name="store_results",
        out_shape=kinds,
        in_specs=[pl.BlockSpec(memory_space=pltpu.VMEM)] * 5,
        out_specs=(pl.BlockSpec(memory_space=pltpu.VMEM),) * 5,
        compiler_params=pltpu.CompilerParams(vmem_limit_bytes=32 << 20),
    )(*results)
    return (
        grad_q[None], grad_k[None], grad_v[None], grad_qg.reshape(HD), grad_kg.reshape(HD)
    )


def solution(mesh):
    tokens = P("dp", "seq", None, None)
    return jax.shard_map(
        body,
        mesh=mesh,
        in_specs=(tokens, tokens, tokens, tokens, P("dp", "seq"), P(), P()),
        out_specs=(tokens, tokens, tokens, P(), P()),
        check_vma=False,
    )
```
